32 devices in a mesh: groups: 2 (over y), col: 4 (over z), row: 2 (over x), head: 2 (over core).
Axes of the slice: x: 2, y: 2, z: 4, core: 2. Of those that a mesh axis runs over, the one named last changes fastest.
Arguments:
- pair: bfloat16 [4, 512, 128], P(('groups', 'row'), 'col'), parts along dimension 0, may hold values from -24 to 24
- out_grad: bfloat16 [4, 512, 128], P(('groups', 'row'), 'col'), parts along dimension 0, may hold values from -400 to 400
- pair_bias: bfloat16 [1024, 4, 512], P(('groups', 'col'), 'head'), parts along dimension 0, may hold values from -6 to 256
- w_query: bfloat16 [128, 128], P(None, 'head'), may hold values from -0.5 to 0.5
- w_key: bfloat16 [128, 128], P(None, 'head'), may hold values from -0.5 to 0.5
- w_value: bfloat16 [128, 128], P(None, 'head'), may hold values from -0.5 to 0.5
- w_gate: bfloat16 [128, 128], P(None, 'head'), may hold values from -0.5 to 0.5
- w_out: bfloat16 [128, 128], P('head'), may hold values from -0.5 to 0.5
- tile_mask: int32 [8, 4], P('groups'), parts along dimension 0, may hold values from 0 to 1, as said below
- chain_ids: int32 [1024], P('groups'), parts along dimension 0, may hold values from 0 to 7, never falling along the last dimension, each value on 1 to 128 neighbouring positions
Outputs:
- pair_grad: bfloat16 [4, 512, 128], P(('groups', 'row'), ('col', 'head')), parts along dimension 0
- query_weight_grad: float32 [256, 128], P('groups', 'head'), parts along dimension 0
- key_weight_grad: float32 [256, 128], P('groups', 'head'), parts along dimension 0
- value_weight_grad: float32 [256, 128], P('groups', 'head'), parts along dimension 0
- gate_weight_grad: float32 [256, 128], P('groups', 'head'), parts along dimension 0
- out_weight_grad: float32 [256, 128], P(('groups', 'head')), parts along dimension 0
The draws below stay inside these ranges and needn't reach their ends.
There are 2 independent parts, one for each index of `groups`. The reference program is written for one: setup_inputs(seed, part) draws one part's arguments, and reference() takes and returns one part's arrays. A program takes and returns all parts, laid end to end along the dimension named above; an argument that names none is the same for every part. Nothing has to cross between parts.
Inputs may be any that keep to these rules, and one draw needn't show every extreme that they name: `tile_mask`: 1 where the residues of a query tile and a key tile, each of 128 residues, may attend to each other.
All inputs are finite; a program needn't handle non-finite values.
Results may differ from the reference program's by a relative error of at most 0.03.
The reference program's roundings to bfloat16 on the way count: a program that leaves them out, or rounds other values in their place, can miss the bound.
Values may be sent and summed in bfloat16 or wider, within the bound.
No kernel may reach another device: no remote copies, remote signals or barrier semaphores. Data moves between devices by JAX's collectives and lax.ppermute only.
A program may use at most 64 MiB of HBM per device.

```python
import math
import jax
import jax.numpy as jnp
import numpy as np
from jax import lax

C = 128
H = 4
HD = 32
TILE = 128
CHAINS = 8
SLAB = 2
N = 512
NT = 4


def draw_pair(key, part):
    noise_key, scale_key = jax.random.split(jax.random.fold_in(key, 11), 2)
    channel_scale = jnp.exp(jax.random.uniform(scale_key, (C,), jnp.float32, math.log(0.3), math.log(3.0)))
    values = jax.random.truncated_normal(noise_key, -6.0, 6.0, (SLAB, N, C), jnp.float32) * channel_scale
    return values.astype(jnp.bfloat16)


def draw_out_grad(key, part):
    noise_key, scale_key = jax.random.split(jax.random.fold_in(key, 23), 2)
    ramp = 3.0 ** (jnp.arange(N, dtype=jnp.float32) / N)
    column_scale = 2.0 * ramp * jnp.exp(jax.random.uniform(scale_key, (N,), jnp.float32, 0.0, math.log(10.0)))
    values = jax.random.truncated_normal(noise_key, -6.0, 6.0, (SLAB, N, C), jnp.float32)
    return (values * column_scale[None, :, None]).astype(jnp.bfloat16)


def draw_pair_bias(key, part):
    keys_all = jax.random.split(jax.random.fold_in(key, 37), 1)
    values = 1.5 * jax.random.truncated_normal(keys_all[0], -4.0, 4.0, (N, H, N), jnp.float32)
    return values.astype(jnp.bfloat16)


def draw_tile_mask(key, part):
    level_key, pick_key = jax.random.split(jax.random.fold_in(key, 53), 2)
    levels = jax.random.randint(level_key, (1, NT), 1, 9)
    picks = jax.random.randint(pick_key, (NT, NT), 0, 8)
    return (picks < levels).astype(jnp.int32)


def steps_of(own_key, extent, shards, low, top_value):
    level = 1.0
    for dim, blocks in shards:
        heights = jax.random.uniform(jax.random.fold_in(jax.random.fold_in(own_key, 6), dim), (blocks,), jnp.float32, low / len(shards), top_value / len(shards))
        level = level * jnp.repeat(jnp.exp(heights), extent[dim] // blocks).reshape((-1,) + (1,) * (len(extent) - 1 - dim))
    return level


def split_up(number_of, total, reach, slope):
    loads = [(1 << 20) // math.isqrt(rank ** slope) + 1 for rank in range(2, number_of + 1)]
    spare, given = total - reach - (number_of - 1), [1] * (number_of - 1)
    while spare > 0:
        free = [i for i in range(number_of - 1) if given[i] < reach]
        mass, budget = sum([loads[i] for i in free]), spare
        for i in free:
            more = min(reach - given[i], max(1, budget * loads[i] // mass), spare)
            given[i] = given[i] + more
            spare = spare - more
    return np.array([reach] + given)


def uneven(own_key, number_of, total, most, skew):
    if number_of == 2:
        one = jax.random.randint(own_key, (), max(1, total - most), min(most, total - 1) + 1)
        return jnp.stack([one, total - one])
    lengths = jnp.asarray(split_up(number_of, total, most, skew), jnp.int32)
    couples = (number_of - 1) // 2
    donor, taker = lengths[1:1 + 2 * couples:2], lengths[2:2 + 2 * couples:2]
    slack = jnp.minimum(donor - 1, most - taker)
    shifted = jax.random.randint(jax.random.fold_in(own_key, 1), (couples,), 0, 1 << 20) % (slack + 1)
    lengths = lengths.at[1:1 + 2 * couples:2].set(donor - shifted).at[2:2 + 2 * couples:2].set(taker + shifted)
    return lengths[jax.random.permutation(jax.random.fold_in(own_key, 2), number_of)]


def centred(stream_key, extent, spread, most, shards=(), kind=jnp.bfloat16):
    values = spread * jax.random.normal(stream_key, extent, jnp.float32)
    if shards:
        values = values * steps_of(stream_key, extent, shards, -0.22, 0.18)
    return jnp.clip(values, -most, most).astype(kind)


def setup_inputs(seed: int = 0, part: int = 0) -> dict:
    seeds = jax.random.split(jax.random.key(seed), 11)
    own_keys = jax.random.split(jax.random.fold_in(seeds[10], part), 11)
    pair = draw_pair(jax.random.fold_in(jax.random.fold_in(seeds[10], part), 71), part)
    out_grad = draw_out_grad(jax.random.fold_in(jax.random.fold_in(seeds[10], part), 71), part)
    pair_bias = draw_pair_bias(jax.random.fold_in(jax.random.fold_in(seeds[10], part), 71), part)
    w_query = centred(seeds[3], (C, H * HD), C ** -0.5, 0.5, ((1, 2),))
    w_key = centred(seeds[4], (C, H * HD), C ** -0.5, 0.5, ((1, 2),))
    w_value = centred(seeds[5], (C, H * HD), C ** -0.5, 0.5, ((1, 2),))
    w_gate = centred(seeds[6], (C, H * HD), C ** -0.5, 0.5, ((1, 2),))
    w_out = centred(seeds[7], (H * HD, C), (H * HD) ** -0.5, 0.5, ((0, 2),))
    tile_mask = draw_tile_mask(jax.random.fold_in(jax.random.fold_in(seeds[10], part), 71), part)
    chain_ids = jnp.searchsorted(jnp.cumsum(uneven(own_keys[9], CHAINS, N, N // 4, 2)), jnp.arange(N), side="right").astype(jnp.int32)
    return {"pair": pair, "out_grad": out_grad, "pair_bias": pair_bias, "w_query": w_query, "w_key": w_key, "w_value": w_value, "w_gate": w_gate, "w_out": w_out, "tile_mask": tile_mask, "chain_ids": chain_ids}


NEG_FILL = -1e+30

def allowed_pairs(tile_mask, chain_ids):
    position = jnp.arange(N, dtype=jnp.int32)
    tile_of = position // TILE
    marks = tile_mask[tile_of][:, tile_of]
    return (marks == 1) | (chain_ids[:, None] == chain_ids[None, :])

def heads_first(flat_rows):
    return flat_rows.reshape(SLAB, N, H, HD).transpose(0, 2, 1, 3)

def heads_last(stacked):
    return stacked.reshape(SLAB, H, N, HD).transpose(0, 2, 1, 3).reshape(SLAB * N, H * HD)

def reference(pair, out_grad, pair_bias, w_query, w_key, w_value, w_gate, w_out, tile_mask, chain_ids):
    hd_scale = HD ** (-0.5)
    flat_pair = pair.reshape(SLAB * N, C)
    flat_grad = out_grad.reshape(SLAB * N, C)
    query_all = heads_first((jnp.dot(flat_pair, w_query, preferred_element_type=jnp.float32) * hd_scale).astype(jnp.bfloat16))
    key_all = heads_first(jnp.dot(flat_pair, w_key, preferred_element_type=jnp.float32).astype(jnp.bfloat16))
    value_all = heads_first(jnp.dot(flat_pair, w_value, preferred_element_type=jnp.float32).astype(jnp.bfloat16))
    gate_all = heads_first(jax.nn.sigmoid(jnp.dot(flat_pair, w_gate, preferred_element_type=jnp.float32)))
    grad_gated_all = heads_first(jnp.dot(flat_grad, w_out.T, preferred_element_type=jnp.float32))
    allowed = allowed_pairs(tile_mask, chain_ids)

    def one_slice(flat_index):
        row_index = flat_index // H
        head_index = flat_index % H
        query_h = query_all[row_index, head_index]
        key_h = key_all[row_index, head_index]
        value_h = value_all[row_index, head_index]
        gate_h = gate_all[row_index, head_index]
        grad_h = grad_gated_all[row_index, head_index]
        bias_h = lax.dynamic_index_in_dim(pair_bias, head_index, 1, keepdims=False).astype(jnp.float32)
        scores = jnp.dot(query_h, key_h.T, preferred_element_type=jnp.float32) + bias_h
        scores = jnp.where(allowed, scores, NEG_FILL)
        row_max = lax.optimization_barrier(jnp.max(scores, axis=1, keepdims=True))
        expo = jnp.where(allowed, jnp.exp(scores - row_max), 0.0)
        row_sum = lax.optimization_barrier(jnp.sum(expo, axis=1, keepdims=True))
        attended = jnp.dot(expo.astype(jnp.bfloat16), value_h, preferred_element_type=jnp.float32) / row_sum
        gated = (gate_h * attended).astype(jnp.bfloat16)
        grad_att = (grad_h * gate_h).astype(jnp.bfloat16)
        grad_gate_logit = (grad_h * attended * gate_h * (1.0 - gate_h)).astype(jnp.bfloat16)
        delta = lax.optimization_barrier(jnp.sum(grad_att.astype(jnp.float32) * attended, axis=1, keepdims=True))
        log_total = row_max + jnp.log(row_sum)
        prob = jnp.where(allowed, jnp.exp(scores - log_total), 0.0)
        grad_prob = jnp.dot(grad_att, value_h.T, preferred_element_type=jnp.float32)
        grad_score = (prob * (grad_prob - delta)).astype(jnp.bfloat16)
        grad_query = (jnp.dot(grad_score, key_h, preferred_element_type=jnp.float32) * hd_scale).astype(jnp.bfloat16)
        grad_key = jnp.dot(grad_score.T, query_h, preferred_element_type=jnp.float32).astype(jnp.bfloat16)
        grad_value = jnp.dot(prob.astype(jnp.bfloat16).T, grad_att, preferred_element_type=jnp.float32).astype(jnp.bfloat16)
        return (gated, grad_query, grad_key, grad_value, grad_gate_logit)
    results = lax.map(one_slice, jnp.arange(SLAB * H, dtype=jnp.int32))
    gated_flat = heads_last(results[0])
    grad_joined = jnp.concatenate([heads_last(results[1]), heads_last(results[2]), heads_last(results[3]), heads_last(results[4])], axis=1)
    w_joined = jnp.concatenate([w_query, w_key, w_value, w_gate], axis=1)
    pair_grad = jnp.dot(grad_joined, w_joined.T, preferred_element_type=jnp.float32).astype(jnp.bfloat16).reshape(SLAB, N, C)
    raw_four = jnp.dot(flat_pair.T, grad_joined, preferred_element_type=jnp.float32)
    raw_out = jnp.dot(gated_flat.T, flat_grad, preferred_element_type=jnp.float32)
    squares = jnp.sum(raw_four * raw_four) + jnp.sum(raw_out * raw_out)
    clip = jnp.minimum(1.0, 0.5 * math.sqrt(5.0 * C * H * HD) / jnp.sqrt(squares + 1e-06))
    head_width = H * HD
    return (pair_grad, raw_four[:, :head_width] * clip, raw_four[:, head_width:2 * head_width] * clip, raw_four[:, 2 * head_width:3 * head_width] * clip, raw_four[:, 3 * head_width:] * clip, raw_out * clip)
```

```python
import math

import jax
import jax.numpy as jnp
from jax import lax
from jax.experimental import pallas as pl
from jax.experimental.pallas import tpu as pltpu
from jax.sharding import PartitionSpec as P

C = 128
H = 4
HD = 32
TILE = 128


NEG_FILL = -1e30
F32 = jnp.float32
BF16 = jnp.bfloat16
CLIP_NORM = 0.5 * math.sqrt(5.0 * C * H * HD)

def shifted(value, axis, steps):
    count = lax.axis_size(axis)
    pairs = [(source, (source + steps) % count) for source in range(count)]
    return lax.ppermute(value, axis, pairs)


def allowed_between(tile_mask, chain_ids, query_start, query_count, key_start, key_count):
    tile_ids = jnp.arange(tile_mask.shape[0], dtype=jnp.int32)
    query_pos = query_start + jnp.arange(query_count, dtype=jnp.int32)
    key_pos = key_start + jnp.arange(key_count, dtype=jnp.int32)
    query_tiles = (query_pos[:, None] // TILE == tile_ids[None, :]).astype(jnp.float32)
    key_tiles = (key_pos[:, None] // TILE == tile_ids[None, :]).astype(jnp.float32)
    marks = jnp.dot(jnp.dot(query_tiles, tile_mask.astype(jnp.float32)), key_tiles.T)
    query_chain = lax.dynamic_slice_in_dim(chain_ids, query_start, query_count)
    key_chain = lax.dynamic_slice_in_dim(chain_ids, key_start, key_count)
    return (marks > 0.5) | (query_chain[:, None] == key_chain[None, :])


def score_block(query_four, key_four, bias_block, allowed):
    scores = jnp.einsum("rjhd,rkhd->rjhk", query_four, key_four, preferred_element_type=jnp.float32)
    scores = scores + bias_block[None].astype(jnp.float32)
    return jnp.where(allowed[None, :, None, :], scores, NEG_FILL)


def prob_and_grad(
    query_four, grad_four, log_total, delta_sum, key_four, value_four, bias_block, allowed
):
    scores = score_block(query_four, key_four, bias_block, allowed)
    prob = jnp.where(allowed[None, :, None, :], jnp.exp(scores - log_total[..., None]), 0.0)
    grad_prob = jnp.einsum(
        "rjhd,rkhd->rjhk", grad_four, value_four, preferred_element_type=jnp.float32
    )
    grad_score = (prob * (grad_prob - delta_sum[..., None])).astype(jnp.bfloat16)
    return (prob.astype(jnp.bfloat16), grad_score)


def any_cols(
    pair, out_grad, pair_bias, w_query, w_key, w_value, w_gate, w_out, tile_mask, chain_ids
):
    rows_dev, cols_dev, channels = pair.shape
    heads_dev = pair_bias.shape[1]
    head_width = w_query.shape[1]
    head_size = head_width // heads_dev
    hd_scale = head_size ** (-0.5)
    col_count = lax.axis_size("col")
    col_index = lax.axis_index("col")
    col_start = col_index * cols_dev
    shape_four = (rows_dev, cols_dev, heads_dev, head_size)
    stat_shape = (rows_dev, cols_dev, heads_dev)
    flat_pair = pair.reshape(rows_dev * cols_dev, channels)
    flat_grad = out_grad.reshape(rows_dev * cols_dev, channels)
    w_joined = jnp.concatenate([w_query, w_key, w_value, w_gate], axis=1)
    projected = jnp.dot(flat_pair, w_joined, preferred_element_type=jnp.float32)
    query_flat = (projected[:, :head_width] * hd_scale).astype(jnp.bfloat16)
    key_grid = (
        projected[:, head_width : 2 * head_width]
        .astype(jnp.bfloat16)
        .reshape(rows_dev, cols_dev, head_width)
    )
    value_grid = (
        projected[:, 2 * head_width : 3 * head_width]
        .astype(jnp.bfloat16)
        .reshape(rows_dev, cols_dev, head_width)
    )
    gate_value = jax.nn.sigmoid(projected[:, 3 * head_width :])
    query_four = query_flat.reshape(shape_four)
    key_piece = lax.all_gather(key_grid, "col", axis=1, tiled=True)
    value_piece = lax.all_gather(value_grid, "col", axis=1, tiled=True)
    key_count = key_piece.shape[1]
    allowed = allowed_between(tile_mask, chain_ids, col_start, cols_dev, jnp.int32(0), key_count)
    bias_block = pair_bias
    run_max = jnp.full(stat_shape, NEG_FILL, jnp.float32)
    key_four = key_piece.reshape(rows_dev, key_count, heads_dev, head_size)
    value_four = value_piece.reshape(rows_dev, key_count, heads_dev, head_size)
    scores = score_block(query_four, key_four, bias_block, allowed)
    new_max = jnp.maximum(run_max, jnp.max(scores, axis=3))
    weights = jnp.where(allowed[None, :, None, :], jnp.exp(scores - new_max[..., None]), 0.0)
    new_sum = jnp.sum(weights, axis=3)
    added = jnp.einsum(
        "rjhk,rkhd->rjhd",
        weights.astype(jnp.bfloat16),
        value_four,
        preferred_element_type=jnp.float32,
    )
    attended = (added / new_sum[..., None]).reshape(rows_dev * cols_dev, head_width)
    log_total = new_max + jnp.log(new_sum)
    gated = (gate_value * attended).astype(jnp.bfloat16)
    grad_gated = jnp.dot(flat_grad, w_out.T, preferred_element_type=jnp.float32)
    grad_att = (grad_gated * gate_value).astype(jnp.bfloat16)
    grad_gate_logit = (grad_gated * attended * gate_value * (1.0 - gate_value)).astype(jnp.bfloat16)
    delta_sum = jnp.sum((grad_att.astype(jnp.float32) * attended).reshape(shape_four), axis=3)
    grad_four = grad_att.reshape(shape_four)

    def back_turn(turn_index, loop_state):
        travel_keys, travel_grads, query_acc = loop_state
        owner_col = jnp.mod(col_index - turn_index, col_count)
        key_start = owner_col * cols_dev
        allowed = allowed_between(tile_mask, chain_ids, col_start, cols_dev, key_start, cols_dev)
        bias_block = lax.dynamic_slice_in_dim(pair_bias, key_start, cols_dev, 2)
        grads_in = travel_grads
        query_in = query_acc
        key_four = travel_keys[0].reshape(shape_four)
        value_four = travel_keys[1].reshape(shape_four)
        prob_bf, grad_score = prob_and_grad(
            query_four, grad_four, log_total, delta_sum, key_four, value_four, bias_block, allowed
        )
        query_more = jnp.einsum(
            "rjhk,rkhd->rjhd", grad_score, key_four, preferred_element_type=jnp.float32
        )
        key_more = jnp.einsum(
            "rjhk,rjhd->rkhd", grad_score, query_four, preferred_element_type=jnp.float32
        )
        value_more = jnp.einsum(
            "rjhk,rjhd->rkhd", prob_bf, grad_four, preferred_element_type=jnp.float32
        )
        travel_grads = grads_in + jnp.stack([key_more, value_more]).reshape(grads_in.shape)
        query_acc = query_in + query_more
        travel_keys = shifted(travel_keys, "col", 1)
        travel_grads = shifted(travel_grads.astype(jnp.bfloat16), "col", 1).astype(
            travel_grads.dtype
        )
        return (travel_keys, travel_grads, query_acc)

    def back_pair(pair_index, loop_state):
        for half_turn in range(2):
            loop_state = back_turn(2 * pair_index + half_turn, loop_state)
        return loop_state

    loop_start = (
        jnp.stack([key_grid, value_grid]),
        jnp.zeros((2, rows_dev, cols_dev, head_width), jnp.float32),
        jnp.zeros(shape_four, jnp.float32),
    )
    travel_keys, key_value_acc, query_acc = lax.fori_loop(0, col_count // 2, back_pair, loop_start)
    query_grad = (
        (query_acc * hd_scale).astype(jnp.bfloat16).reshape(rows_dev * cols_dev, head_width)
    )
    key_grad = key_value_acc[0].astype(jnp.bfloat16).reshape(rows_dev * cols_dev, head_width)
    value_grad = key_value_acc[1].astype(jnp.bfloat16).reshape(rows_dev * cols_dev, head_width)
    grad_joined = jnp.concatenate([query_grad, key_grad, value_grad, grad_gate_logit], axis=1)
    partial_pair = jnp.dot(grad_joined, w_joined.T, preferred_element_type=jnp.float32).reshape(
        rows_dev, cols_dev, channels
    )
    pair_grad = lax.psum_scatter(
        partial_pair.astype(jnp.bfloat16), "head", scatter_dimension=1, tiled=True
    )
    raw_four = jnp.dot(flat_pair.T, grad_joined, preferred_element_type=jnp.float32)
    raw_out = jnp.dot(gated.T, flat_grad, preferred_element_type=jnp.float32)
    summed_four, summed_out = lax.psum((raw_four, raw_out), ("col", "row"))
    local_squares = jnp.sum(summed_four * summed_four) + jnp.sum(summed_out * summed_out)
    squares = lax.psum(local_squares, "head")
    clip = jnp.minimum(1.0, 0.5 * math.sqrt(5.0 * C * H * HD) / jnp.sqrt(squares + 1e-06))
    return (
        pair_grad,
        summed_four[:, :head_width] * clip,
        summed_four[:, head_width : 2 * head_width] * clip,
        summed_four[:, 2 * head_width : 3 * head_width] * clip,
        summed_four[:, 3 * head_width :] * clip,
        summed_out * clip,
    )


def crossed(value, axis, bits):
    count = lax.axis_size(axis)
    return lax.ppermute(value, axis, [(source, source ^ bits) for source in range(count)])


def dot_nn(left, right):
    return jnp.dot(left, right, preferred_element_type=F32)


def dot_nt(left, right):
    return lax.dot_general(left, right, (((1,), (1,)), ((), ())), preferred_element_type=F32)


def split_rows(flat):
    first = lax.broadcasted_iota(jnp.int32, flat.shape, 0) < HD
    zero = jnp.zeros_like(flat)
    return jnp.concatenate([jnp.where(first, flat, zero), jnp.where(first, zero, flat)], axis=1)


def join_rows(wide):
    count = wide.shape[1] // 2
    first = lax.broadcasted_iota(jnp.int32, (wide.shape[0], count), 0) < HD
    return jnp.where(first, wide[:, :count], wide[:, count:])


def split_cols(flat):
    first = lax.broadcasted_iota(jnp.int32, flat.shape, 1) < HD
    zero = jnp.zeros_like(flat)
    return jnp.concatenate([jnp.where(first, flat, zero), jnp.where(first, zero, flat)], axis=0)


def attention_kernel(
    col_ref, x_ref, x1_ref, x2_ref, x3_ref, grad_ref, bias_ref,
    wq_ref, wk_ref, wv_ref, wg_ref, wo_ref,
    raw_ref, keep_ref, send_ref,
    pairs_ref, scores_ref, expo_ref, both_ref, parts_ref,
):
    scale = HD ** (-0.5)
    width = 2 * TILE
    me = col_ref[0]
    places = [pl.multiple_of(lax.bitwise_xor(me, bits) * TILE, TILE) for bits in range(4)]
    x = x_ref[...]
    for place, ref in zip(places, (x_ref, x1_ref, x2_ref, x3_ref)):
        pairs_ref[pl.ds(place, TILE), :] = ref[...]
    out_grad = grad_ref[...]
    w_q, w_g, w_o = wq_ref[...], wg_ref[...], wo_ref[...]
    w_kv = jnp.concatenate([wk_ref[...], wv_ref[...]], axis=0)
    w_qg = jnp.concatenate([w_q, w_g], axis=0)

    query_gate = dot_nt(w_qg, x)
    query_t = (query_gate[: 2 * HD] * scale).astype(BF16)
    gate_t = jax.nn.sigmoid(query_gate[2 * HD :])
    query = (dot_nt(x, w_q) * scale).astype(BF16)
    gated_grad_t = dot_nt(w_o, out_grad)
    att_grad_f = (gated_grad_t * gate_t).astype(BF16).astype(F32)
    att_grad_t = att_grad_f.astype(BF16)
    att_grad = jnp.transpose(att_grad_f).astype(BF16)

    pairs = pairs_ref[...]
    key_value = dot_nt(pairs, w_kv).astype(BF16)
    key_value_t = dot_nt(w_kv, pairs).astype(BF16)
    zero_wide = jnp.zeros((2 * HD, width), BF16)
    left = jnp.concatenate(
        [
            jnp.concatenate([split_rows(query_t), zero_wide], axis=1),
            jnp.concatenate([zero_wide, split_rows(att_grad_t)], axis=1),
        ],
        axis=0,
    )
    top = None
    for block in range(4):
        rows = slice(block * TILE, (block + 1) * TILE)
        product = dot_nn(key_value[rows], left)
        scores = product[:, :width] + bias_ref[rows, :].astype(F32)
        scores_ref[rows, :width] = scores
        scores_ref[rows, width:] = product[:, width:]
        part = jnp.max(scores.reshape(TILE // 8, 8, width), axis=0)
        top = part if top is None else jnp.maximum(top, part)
    top = jnp.max(top, axis=0, keepdims=True)
    total = jnp.zeros((8, width), F32)
    for block in range(4):
        rows = slice(block * TILE, (block + 1) * TILE)
        expo = jnp.exp(scores_ref[rows, :width] - top)
        scores_ref[rows, :width] = expo
        expo_ref[rows, :] = expo.astype(BF16)
        total = total + jnp.sum(expo.reshape(TILE // 8, 8, width), axis=0)
    total = jnp.sum(total, axis=0, keepdims=True)
    inverse = 1.0 / total
    attended_t = join_rows(dot_nn(key_value_t[2 * HD :], expo_ref[...]) * inverse)
    gated_t = (gate_t * attended_t).astype(BF16)
    gate_logit_t = gated_grad_t * attended_t * gate_t * (1.0 - gate_t)
    products = att_grad_f * attended_t
    delta = jnp.concatenate(
        [
            jnp.sum(products[:HD], axis=0, keepdims=True),
            jnp.sum(products[HD:], axis=0, keepdims=True),
        ],
        axis=1,
    )
    for block in range(4):
        rows = slice(block * TILE, (block + 1) * TILE)
        prob = scores_ref[rows, :width] * inverse
        both_ref[rows, :width] = (prob * (scores_ref[rows, width:] - delta)).astype(BF16)
        both_ref[rows, width:] = prob.astype(BF16)
    query_grad_t = join_rows(dot_nn(key_value_t[: 2 * HD], both_ref[:, :width])) * scale
    zero_tall = jnp.zeros((width, 2 * HD), BF16)
    right = jnp.concatenate(
        [
            jnp.concatenate([split_cols(query), zero_tall], axis=1),
            jnp.concatenate([zero_tall, split_cols(att_grad)], axis=1),
        ],
        axis=0,
    )
    key_value_grad = dot_nn(both_ref[...], right)
    local_t = jnp.concatenate([query_grad_t, gate_logit_t], axis=0)
    local = jnp.transpose(local_t).astype(BF16)
    parts_ref[...] = dot_nn(key_value_grad.astype(BF16), w_kv)
    own = pl.ds(places[0], TILE)
    parts_ref[own, :] = parts_ref[own, :] + dot_nn(local, w_qg)
    keep_ref[:TILE, :] = parts_ref[own, :].astype(BF16)
    keep_ref[TILE:, :] = parts_ref[pl.ds(places[1], TILE), :].astype(BF16)
    send_ref[:TILE, :] = parts_ref[pl.ds(places[2], TILE), :].astype(BF16)
    send_ref[TILE:, :] = parts_ref[pl.ds(places[3], TILE), :].astype(BF16)
    raw_ref[: 4 * HD, :] = dot_nn(local_t.astype(BF16), x).astype(BF16)
    raw_ref[4 * HD : 8 * HD, :] = dot_nn(jnp.transpose(key_value_grad).astype(BF16), pairs).astype(BF16)
    raw_ref[8 * HD :, :] = dot_nn(gated_t, out_grad).astype(BF16)


def attention(col_index, xs, out_grad, bias, weights):
    spec = pl.BlockSpec(memory_space=pltpu.VMEM)
    keys = 4 * TILE
    return pl.pallas_call(
        attention_kernel,
        out_shape=(
            jax.ShapeDtypeStruct((10 * HD, C), BF16),
            jax.ShapeDtypeStruct((2 * TILE, C), BF16),
            jax.ShapeDtypeStruct((2 * TILE, C), BF16),
        ),
        in_specs=[pl.BlockSpec(memory_space=pltpu.SMEM)] + [spec] * 11,
        out_specs=(spec, spec, spec),
        scratch_shapes=[
            pltpu.VMEM((keys, C), BF16),
            pltpu.VMEM((keys, 4 * TILE), F32),
            pltpu.VMEM((keys, 2 * TILE), BF16),
            pltpu.VMEM((keys, 4 * TILE), BF16),
            pltpu.VMEM((keys, C), F32),
        ],
        name="attention",
    )(col_index.reshape(1), *xs, out_grad, bias, *weights)


def masked_bias(pair_bias, tile_mask, chain_ids, col_index):
    keys = chain_ids.shape[0]
    marks = jnp.repeat(lax.dynamic_index_in_dim(tile_mask, col_index, 0, keepdims=False), TILE)
    own_chain = lax.dynamic_slice_in_dim(chain_ids, col_index * TILE, TILE)
    allowed = (marks[:, None] == 1) | (chain_ids[:, None] == own_chain[None, :])
    turned = jnp.transpose(pair_bias, (2, 1, 0))
    masked = jnp.where(allowed[:, None, :], turned, jnp.asarray(NEG_FILL, BF16))
    return masked.reshape(keys, 2 * TILE)


def four_cols(
    pair, out_grad, pair_bias, w_query, w_key, w_value, w_gate, w_out, tile_mask, chain_ids
):
    col_index = lax.axis_index("col")
    head_index = lax.axis_index("head")
    x = pair.reshape(TILE, C)
    x2 = crossed(x, "col", 2)
    x1 = crossed(x, "col", 1)
    x3 = crossed(x2, "col", 1)
    bias = masked_bias(pair_bias, tile_mask, chain_ids, col_index)
    raw, keep, send = attention(
        col_index,
        (x, x1, x2, x3),
        out_grad.reshape(TILE, C),
        bias,
        (w_query.T, w_key.T, w_value.T, w_gate.T, w_out),
    )
    row_raw = crossed(raw, "row", 1)
    two_parts = keep.astype(F32) + crossed(send, "col", 2).astype(F32)
    raw = (raw.astype(F32) + row_raw.astype(F32)).astype(BF16)
    raw = (raw.astype(F32) + crossed(raw, "col", 2).astype(F32)).astype(BF16)
    one_part = two_parts[:TILE] + crossed(two_parts[TILE:].astype(BF16), "col", 1).astype(F32)
    raw = raw.astype(F32) + crossed(raw, "col", 1).astype(F32)
    half = TILE // 2
    mine = lax.dynamic_slice_in_dim(one_part, head_index * half, half, 0)
    other = lax.dynamic_slice_in_dim(one_part, (1 - head_index) * half, half, 0)
    pair_grad = (mine + crossed(other.astype(BF16), "head", 1).astype(F32)).astype(BF16)
    squares = jnp.sum(raw * raw).reshape(1, 1)
    squares = squares + crossed(squares, "head", 1)
    clip = jnp.minimum(1.0, CLIP_NORM / jnp.sqrt(squares + 1e-06))
    raw = raw * clip
    width = 2 * HD
    return (
        pair_grad.reshape(1, half, C),
        raw[:width].T,
        raw[2 * width : 3 * width].T,
        raw[3 * width : 4 * width].T,
        raw[width : 2 * width].T,
        raw[4 * width :],
    )


def per_device(pair, out_grad, pair_bias, *rest):
    small = lax.axis_size("col") == 4 and lax.axis_size("row") == 2 and lax.axis_size("head") == 2
    if small and pair.shape == (1, TILE, C) and pair_bias.shape == (TILE, 2, 4 * TILE):
        return four_cols(pair, out_grad, pair_bias, *rest)
    return any_cols(pair, out_grad, pair_bias, *rest)


def solution(mesh):
    return jax.shard_map(
        per_device,
        mesh=mesh,
        in_specs=(
            P(("groups", "row"), "col", None),
            P(("groups", "row"), "col", None),
            P(("groups", "col"), "head", None),
            P(None, "head"),
            P(None, "head"),
            P(None, "head"),
            P(None, "head"),
            P("head", None),
            P("groups", None),
            P("groups"),
        ),
        out_specs=(
            P(("groups", "row"), ("col", "head"), None),
            P("groups", "head"),
            P("groups", "head"),
            P("groups", "head"),
            P("groups", "head"),
            P(("groups", "head"), None),
        ),
        check_vma=False,
    )
```

```python
import math

import jax
import jax.numpy as jnp
from jax import lax
from jax.experimental import pallas as pl
from jax.experimental.pallas import tpu as pltpu
from jax.sharding import PartitionSpec as P

C = 128
H = 4
HD = 32
TILE = 128


NEG_FILL = -1e30
F32 = jnp.float32
BF16 = jnp.bfloat16
CLIP_NORM = 0.5 * math.sqrt(5.0 * C * H * HD)


def shifted(value, axis, steps):
    count = lax.axis_size(axis)
    pairs = [(source, (source + steps) % count) for source in range(count)]
    return lax.ppermute(value, axis, pairs)


def allowed_between(tile_mask, chain_ids, query_start, query_count, key_start, key_count):
    tile_ids = jnp.arange(tile_mask.shape[0], dtype=jnp.int32)
    query_pos = query_start + jnp.arange(query_count, dtype=jnp.int32)
    key_pos = key_start + jnp.arange(key_count, dtype=jnp.int32)
    query_tiles = (query_pos[:, None] // TILE == tile_ids[None, :]).astype(jnp.float32)
    key_tiles = (key_pos[:, None] // TILE == tile_ids[None, :]).astype(jnp.float32)
    marks = jnp.dot(jnp.dot(query_tiles, tile_mask.astype(jnp.float32)), key_tiles.T)
    query_chain = lax.dynamic_slice_in_dim(chain_ids, query_start, query_count)
    key_chain = lax.dynamic_slice_in_dim(chain_ids, key_start, key_count)
    return (marks > 0.5) | (query_chain[:, None] == key_chain[None, :])


def score_block(query_four, key_four, bias_block, allowed):
    scores = jnp.einsum("rjhd,rkhd->rjhk", query_four, key_four, preferred_element_type=jnp.float32)
    scores = scores + bias_block[None].astype(jnp.float32)
    return jnp.where(allowed[None, :, None, :], scores, NEG_FILL)


def prob_and_grad(
    query_four, grad_four, log_total, delta_sum, key_four, value_four, bias_block, allowed
):
    scores = score_block(query_four, key_four, bias_block, allowed)
    prob = jnp.where(allowed[None, :, None, :], jnp.exp(scores - log_total[..., None]), 0.0)
    grad_prob = jnp.einsum(
        "rjhd,rkhd->rjhk", grad_four, value_four, preferred_element_type=jnp.float32
    )
    grad_score = (prob * (grad_prob - delta_sum[..., None])).astype(jnp.bfloat16)
    return (prob.astype(jnp.bfloat16), grad_score)


def any_cols(
    pair, out_grad, pair_bias, w_query, w_key, w_value, w_gate, w_out, tile_mask, chain_ids
):
    rows_dev, cols_dev, channels = pair.shape
    heads_dev = pair_bias.shape[1]
    head_width = w_query.shape[1]
    head_size = head_width // heads_dev
    hd_scale = head_size ** (-0.5)
    col_count = lax.axis_size("col")
    col_index = lax.axis_index("col")
    col_start = col_index * cols_dev
    shape_four = (rows_dev, cols_dev, heads_dev, head_size)
    stat_shape = (rows_dev, cols_dev, heads_dev)
    flat_pair = pair.reshape(rows_dev * cols_dev, channels)
    flat_grad = out_grad.reshape(rows_dev * cols_dev, channels)
    w_joined = jnp.concatenate([w_query, w_key, w_value, w_gate], axis=1)
    projected = jnp.dot(flat_pair, w_joined, preferred_element_type=jnp.float32)
    query_flat = (projected[:, :head_width] * hd_scale).astype(jnp.bfloat16)
    key_grid = (
        projected[:, head_width : 2 * head_width]
        .astype(jnp.bfloat16)
        .reshape(rows_dev, cols_dev, head_width)
    )
    value_grid = (
        projected[:, 2 * head_width : 3 * head_width]
        .astype(jnp.bfloat16)
        .reshape(rows_dev, cols_dev, head_width)
    )
    gate_value = jax.nn.sigmoid(projected[:, 3 * head_width :])
    query_four = query_flat.reshape(shape_four)
    key_piece = lax.all_gather(key_grid, "col", axis=1, tiled=True)
    value_piece = lax.all_gather(value_grid, "col", axis=1, tiled=True)
    key_count = key_piece.shape[1]
    allowed = allowed_between(tile_mask, chain_ids, col_start, cols_dev, jnp.int32(0), key_count)
    bias_block = pair_bias
    run_max = jnp.full(stat_shape, NEG_FILL, jnp.float32)
    key_four = key_piece.reshape(rows_dev, key_count, heads_dev, head_size)
    value_four = value_piece.reshape(rows_dev, key_count, heads_dev, head_size)
    scores = score_block(query_four, key_four, bias_block, allowed)
    new_max = jnp.maximum(run_max, jnp.max(scores, axis=3))
    weights = jnp.where(allowed[None, :, None, :], jnp.exp(scores - new_max[..., None]), 0.0)
    new_sum = jnp.sum(weights, axis=3)
    added = jnp.einsum(
        "rjhk,rkhd->rjhd",
        weights.astype(jnp.bfloat16),
        value_four,
        preferred_element_type=jnp.float32,
    )
    attended = (added / new_sum[..., None]).reshape(rows_dev * cols_dev, head_width)
    log_total = new_max + jnp.log(new_sum)
    gated = (gate_value * attended).astype(jnp.bfloat16)
    grad_gated = jnp.dot(flat_grad, w_out.T, preferred_element_type=jnp.float32)
    grad_att = (grad_gated * gate_value).astype(jnp.bfloat16)
    grad_gate_logit = (grad_gated * attended * gate_value * (1.0 - gate_value)).astype(jnp.bfloat16)
    delta_sum = jnp.sum((grad_att.astype(jnp.float32) * attended).reshape(shape_four), axis=3)
    grad_four = grad_att.reshape(shape_four)

    def back_turn(turn_index, loop_state):
        travel_keys, travel_grads, query_acc = loop_state
        owner_col = jnp.mod(col_index - turn_index, col_count)
        key_start = owner_col * cols_dev
        allowed = allowed_between(tile_mask, chain_ids, col_start, cols_dev, key_start, cols_dev)
        bias_block = lax.dynamic_slice_in_dim(pair_bias, key_start, cols_dev, 2)
        grads_in = travel_grads
        query_in = query_acc
        key_four = travel_keys[0].reshape(shape_four)
        value_four = travel_keys[1].reshape(shape_four)
        prob_bf, grad_score = prob_and_grad(
            query_four, grad_four, log_total, delta_sum, key_four, value_four, bias_block, allowed
        )
        query_more = jnp.einsum(
            "rjhk,rkhd->rjhd", grad_score, key_four, preferred_element_type=jnp.float32
        )
        key_more = jnp.einsum(
            "rjhk,rjhd->rkhd", grad_score, query_four, preferred_element_type=jnp.float32
        )
        value_more = jnp.einsum(
            "rjhk,rjhd->rkhd", prob_bf, grad_four, preferred_element_type=jnp.float32
        )
        travel_grads = grads_in + jnp.stack([key_more, value_more]).reshape(grads_in.shape)
        query_acc = query_in + query_more
        travel_keys = shifted(travel_keys, "col", 1)
        travel_grads = shifted(travel_grads.astype(jnp.bfloat16), "col", 1).astype(
            travel_grads.dtype
        )
        return (travel_keys, travel_grads, query_acc)

    def back_pair(pair_index, loop_state):
        for half_turn in range(2):
            loop_state = back_turn(2 * pair_index + half_turn, loop_state)
        return loop_state

    loop_start = (
        jnp.stack([key_grid, value_grid]),
        jnp.zeros((2, rows_dev, cols_dev, head_width), jnp.float32),
        jnp.zeros(shape_four, jnp.float32),
    )
    travel_keys, key_value_acc, query_acc = lax.fori_loop(0, col_count // 2, back_pair, loop_start)
    query_grad = (
        (query_acc * hd_scale).astype(jnp.bfloat16).reshape(rows_dev * cols_dev, head_width)
    )
    key_grad = key_value_acc[0].astype(jnp.bfloat16).reshape(rows_dev * cols_dev, head_width)
    value_grad = key_value_acc[1].astype(jnp.bfloat16).reshape(rows_dev * cols_dev, head_width)
    grad_joined = jnp.concatenate([query_grad, key_grad, value_grad, grad_gate_logit], axis=1)
    partial_pair = jnp.dot(grad_joined, w_joined.T, preferred_element_type=jnp.float32).reshape(
        rows_dev, cols_dev, channels
    )
    pair_grad = lax.psum_scatter(
        partial_pair.astype(jnp.bfloat16), "head", scatter_dimension=1, tiled=True
    )
    raw_four = jnp.dot(flat_pair.T, grad_joined, preferred_element_type=jnp.float32)
    raw_out = jnp.dot(gated.T, flat_grad, preferred_element_type=jnp.float32)
    summed_four, summed_out = lax.psum((raw_four, raw_out), ("col", "row"))
    local_squares = jnp.sum(summed_four * summed_four) + jnp.sum(summed_out * summed_out)
    squares = lax.psum(local_squares, "head")
    clip = jnp.minimum(1.0, 0.5 * math.sqrt(5.0 * C * H * HD) / jnp.sqrt(squares + 1e-06))
    return (
        pair_grad,
        summed_four[:, :head_width] * clip,
        summed_four[:, head_width : 2 * head_width] * clip,
        summed_four[:, 2 * head_width : 3 * head_width] * clip,
        summed_four[:, 3 * head_width :] * clip,
        summed_out * clip,
    )


def exchange(value, partner):
    cols, rows, heads = lax.axis_size("col"), lax.axis_size("row"), lax.axis_size("head")
    pairs = []
    for col in range(cols):
        for row in range(rows):
            for head in range(heads):
                to_col, to_row, to_head = partner(col, row, head)
                source = (col * rows + row) * heads + head
                pairs.append((source, (to_col * rows + to_row) * heads + to_head))
    return lax.ppermute(value, ("col", "row", "head"), pairs)


def next_col(col, row, head):
    return col ^ 1, row, head


def far_col(col, row, head):
    return col ^ 2, row, head


def other_row(col, row, head):
    return col, row ^ 1, head


def other_head(col, row, head):
    return col, row, head ^ 1


def staggered(first, second):
    return lambda col, row, head: (first, second)[head](col, row, head)


def dot_nn(left, right):
    return jnp.dot(left, right, preferred_element_type=F32)


def dot_nt(left, right):
    return lax.dot_general(left, right, (((1,), (1,)), ((), ())), preferred_element_type=F32)


def split_rows(flat):
    first = lax.broadcasted_iota(jnp.int32, flat.shape, 0) < HD
    zero = jnp.zeros_like(flat)
    return jnp.concatenate([jnp.where(first, flat, zero), jnp.where(first, zero, flat)], axis=1)


def join_rows(wide):
    count = wide.shape[1] // 2
    first = lax.broadcasted_iota(jnp.int32, (wide.shape[0], count), 0) < HD
    return jnp.where(first, wide[:, :count], wide[:, count:])


def split_cols(flat):
    first = lax.broadcasted_iota(jnp.int32, flat.shape, 1) < HD
    zero = jnp.zeros_like(flat)
    return jnp.concatenate([jnp.where(first, flat, zero), jnp.where(first, zero, flat)], axis=0)


def local_kernel(
    col_ref, tile_hbm, x_hbm, grad_hbm, bias_hbm, chain_hbm, wq_hbm, wk_hbm, wv_hbm, wg_hbm, wo_hbm,
    x_ref, grad_ref, w_qg_ref, w_kv_ref, bias_out, left_out, right_out, gate_out, gated_grad_out,
    att_grad_out, tile_ref, chain_ref, wo_ref, bias_ref, sems,
):
    scale = HD ** (-0.5)
    width = 2 * TILE
    me = col_ref[0]
    moves = [
        (x_hbm, x_ref),
        (wq_hbm, w_qg_ref.at[: 2 * HD]),
        (wg_hbm, w_qg_ref.at[2 * HD :]),
        (grad_hbm, grad_ref),
        (wo_hbm, wo_ref),
        (chain_hbm, chain_ref),
        (tile_hbm, tile_ref),
        (bias_hbm, bias_ref),
        (wk_hbm, w_kv_ref.at[: 2 * HD]),
        (wv_hbm, w_kv_ref.at[2 * HD :]),
    ]
    copies = [
        pltpu.make_async_copy(source, target, sems.at[place])
        for place, (source, target) in enumerate(moves)
    ]
    for copy in copies:
        copy.start()
    for copy in copies[:5]:
        copy.wait()
    x = x_ref[...]
    query_gate = dot_nt(w_qg_ref[...], x)
    gated_grad_t = dot_nt(wo_ref[...], grad_ref[...])
    query = (dot_nt(x, w_qg_ref[: 2 * HD, :]) * scale).astype(BF16)
    query_t = (query_gate[: 2 * HD] * scale).astype(BF16)
    gate_t = jax.nn.sigmoid(query_gate[2 * HD :])
    att_grad_t = (gated_grad_t * gate_t).astype(BF16)
    att_grad_f = att_grad_t.astype(F32)
    att_grad = jnp.transpose(att_grad_f).astype(BF16)
    zero_wide = jnp.zeros((2 * HD, width), BF16)
    zero_tall = jnp.zeros((width, 2 * HD), BF16)
    left_out[: 2 * HD, :] = jnp.concatenate([split_rows(query_t), zero_wide], axis=1)
    left_out[2 * HD :, :] = jnp.concatenate([zero_wide, split_rows(att_grad_t)], axis=1)
    right_out[:width, :] = jnp.concatenate([split_cols(query), zero_tall], axis=1)
    right_out[width:, :] = jnp.concatenate([zero_tall, split_cols(att_grad)], axis=1)
    gate_out[...] = gate_t
    gated_grad_out[...] = gated_grad_t
    att_grad_out[...] = att_grad_f
    for copy in copies[5:]:
        copy.wait()
    chains = chain_ref[...].astype(F32)
    own_chain = chain_ref[pl.ds(me, 1), :].astype(F32)
    for block in range(4):
        rows = slice(block * TILE, (block + 1) * TILE)
        key_chain = jnp.transpose(jnp.broadcast_to(chains[block : block + 1, :], (TILE, TILE)))
        apart = jnp.where(tile_ref[me, block] == 1, 0.0, 1.0)
        banned = jnp.where(key_chain == own_chain, 0.0, apart) > 0.5
        for head in range(2):
            bias = bias_ref[:, head, rows].astype(F32)
            bias_out[rows, head * TILE : (head + 1) * TILE] = jnp.where(
                banned, NEG_FILL, jnp.transpose(bias)
            )


def attention_kernel(
    col_ref, x_ref, x1_ref, x2_ref, x3_ref, grad_ref, bias_ref, left_ref, right_ref,
    gate_ref, gated_grad_ref, att_grad_ref, w_kv_ref,
    raw_ref, local_ref, key_value_grad_ref,
    pairs_ref, scores_ref, expo_ref, both_ref,
):
    scale = HD ** (-0.5)
    width = 2 * TILE
    me = col_ref[0]
    for bits, ref in enumerate((x_ref, x1_ref, x2_ref, x3_ref)):
        place = pl.multiple_of(lax.bitwise_xor(me, bits) * TILE, TILE)
        pairs_ref[pl.ds(place, TILE), :] = ref[...]
    w_kv = w_kv_ref[...]
    pairs = pairs_ref[...]
    key_value = dot_nt(pairs, w_kv).astype(BF16)
    key_value_t = dot_nt(w_kv, pairs).astype(BF16)
    left = left_ref[...]
    top = None
    for block in range(4):
        rows = slice(block * TILE, (block + 1) * TILE)
        product = dot_nn(key_value[rows], left)
        scores = product[:, :width] + bias_ref[rows, :]
        scores_ref[rows, :width] = scores
        scores_ref[rows, width:] = product[:, width:]
        part = jnp.max(scores.reshape(TILE // 8, 8, width), axis=0)
        top = part if top is None else jnp.maximum(top, part)
    top = jnp.max(top, axis=0, keepdims=True)
    total = jnp.zeros((8, width), F32)
    for block in range(4):
        rows = slice(block * TILE, (block + 1) * TILE)
        expo = jnp.exp(scores_ref[rows, :width] - top)
        scores_ref[rows, :width] = expo
        expo_ref[rows, :] = expo.astype(BF16)
        total = total + jnp.sum(expo.reshape(TILE // 8, 8, width), axis=0)
    inverse = 1.0 / jnp.sum(total, axis=0, keepdims=True)
    attended_t = join_rows(dot_nn(key_value_t[2 * HD :], expo_ref[...]) * inverse)
    gate_t, gated_grad_t = gate_ref[...], gated_grad_ref[...]
    gated_t = (gate_t * attended_t).astype(BF16)
    gate_logit_t = gated_grad_t * attended_t * gate_t * (1.0 - gate_t)
    products = att_grad_ref[...] * attended_t
    delta = jnp.concatenate(
        [
            jnp.sum(products[:HD], axis=0, keepdims=True),
            jnp.sum(products[HD:], axis=0, keepdims=True),
        ],
        axis=1,
    )
    for block in range(4):
        rows = slice(block * TILE, (block + 1) * TILE)
        prob = scores_ref[rows, :width] * inverse
        both_ref[rows, :width] = (prob * (scores_ref[rows, width:] - delta)).astype(BF16)
        both_ref[rows, width:] = prob.astype(BF16)
    query_grad_t = join_rows(dot_nn(key_value_t[: 2 * HD], both_ref[:, :width])) * scale
    key_value_grad = dot_nn(both_ref[...], right_ref[...])
    local_t = jnp.concatenate([query_grad_t, gate_logit_t], axis=0)
    local_ref[...] = jnp.transpose(local_t).astype(BF16)
    key_value_grad_ref[...] = key_value_grad.astype(BF16)
    raw_ref[: 4 * HD, :] = dot_nn(local_t.astype(BF16), x_ref[...]).astype(BF16)
    raw_ref[4 * HD : 8 * HD, :] = dot_nn(jnp.transpose(key_value_grad).astype(BF16), pairs).astype(BF16)
    raw_ref[8 * HD :, :] = dot_nn(gated_t, grad_ref[...]).astype(BF16)


def parts_kernel(
    place_ref, key_value_grad_ref, local_ref, w_qg_ref, w_kv_ref, keep_ref, send_ref, parts_ref
):
    me, head = place_ref[0], place_ref[1]
    half = TILE // 2
    parts_ref[...] = dot_nn(key_value_grad_ref[...], w_kv_ref[...])
    own = pl.ds(pl.multiple_of(me * TILE, TILE), TILE)
    parts_ref[own, :] = parts_ref[own, :] + dot_nn(local_ref[...], w_qg_ref[...])
    for bits in range(4):
        start = lax.bitwise_xor(me, bits) * TILE
        mine = pl.multiple_of(start + head * half, half)
        other = pl.multiple_of(start + (1 - head) * half, half)
        rows = slice(bits * half, (bits + 1) * half)
        keep_ref[rows, :] = parts_ref[pl.ds(mine, half), :]
        send_ref[rows, :] = parts_ref[pl.ds(other, half), :].astype(BF16)


def squares_kernel(own_ref, other_ref, total_ref, squares_ref):
    total = own_ref[...].astype(F32) + other_ref[...].astype(F32)
    total_ref[...] = total
    squares_ref[...] = jnp.sum((total * total).reshape(total.shape[0] // 8, 8, C), axis=0)


def clip_kernel(total_ref, own_ref, other_ref, query_ref, gate_ref, key_ref, value_ref, out_ref):
    squares = own_ref[...] + other_ref[...]
    squares = jnp.sum(jnp.sum(squares, axis=0, keepdims=True), axis=1, keepdims=True)
    clip = jnp.minimum(1.0, CLIP_NORM / jnp.sqrt(squares + 1e-06))
    for part, ref in enumerate((query_ref, gate_ref, key_ref, value_ref, out_ref)):
        ref[...] = total_ref[part * 2 * HD : (part + 1) * 2 * HD, :] * clip


VMEM = pl.BlockSpec(memory_space=pltpu.VMEM)
SMEM = pl.BlockSpec(memory_space=pltpu.SMEM)
HBM = pl.BlockSpec(memory_space=pltpu.HBM)


def on_core(kernel, name, specs, operands, outs, scratch=(), cost=1 << 18):
    return pl.pallas_call(
        kernel,
        out_shape=tuple(jax.ShapeDtypeStruct(shape, dtype) for shape, dtype in outs),
        in_specs=specs + [VMEM] * (len(operands) - len(specs)),
        out_specs=(VMEM,) * len(outs),
        scratch_shapes=scratch,
        compiler_params=pltpu.CompilerParams(vmem_limit_bytes=16 << 20),
        cost_estimate=pl.CostEstimate(flops=1 << 20, bytes_accessed=cost, transcendentals=0),
        name=name,
    )(
        *(
            pltpu.with_memory_space_constraint(operand, pltpu.HBM) if spec is HBM else operand
            for spec, operand in zip(specs + [VMEM] * len(operands), operands)
        )
    )


def four_cols(
    pair, out_grad, pair_bias, w_query, w_key, w_value, w_gate, w_out, tile_mask, chain_ids
):
    col_index = lax.axis_index("col")
    head_index = lax.axis_index("head")
    col = col_index.reshape(1)
    width, keys, wide = 2 * HD, 4 * TILE, 2 * TILE
    x = pair.reshape(TILE, C)
    x2 = exchange(x, far_col)
    x1 = exchange(x, next_col)
    x3 = exchange(x2, next_col)
    x, grad, w_qg, w_kv, bias, left, right, gate_t, gated_grad_t, att_grad_t = on_core(
        local_kernel, "local", [SMEM] + [HBM] * 10,
        (
            col, tile_mask, x, out_grad.reshape(TILE, C), pair_bias, chain_ids.reshape(4, TILE),
            w_query.T, w_key.T, w_value.T, w_gate.T, w_out,
        ),
        (
            ((TILE, C), BF16), ((TILE, C), BF16), ((2 * width, C), BF16), ((2 * width, C), BF16),
            ((keys, wide), F32), ((C, 2 * wide), BF16), ((2 * wide, C), BF16),
            ((width, TILE), F32), ((width, TILE), F32), ((width, TILE), F32),
        ),
        [
            pltpu.SMEM((4, 4), jnp.int32), pltpu.VMEM((4, TILE), jnp.int32),
            pltpu.VMEM((width, C), BF16), pltpu.VMEM((TILE, 2, keys), BF16),
            pltpu.SemaphoreType.DMA((10,)),
        ],
    )
    raw, local, key_value_grad = on_core(
        attention_kernel, "attention", [SMEM],
        (col, x, x1, x2, x3, grad, bias, left, right, gate_t, gated_grad_t, att_grad_t, w_kv),
        (((5 * width, C), BF16), ((TILE, C), BF16), ((keys, C), BF16)),
        [
            pltpu.VMEM((keys, C), BF16), pltpu.VMEM((keys, 2 * wide), F32),
            pltpu.VMEM((keys, wide), BF16), pltpu.VMEM((keys, 2 * wide), BF16),
        ],
    )

    def summed(one, two):
        return (one.astype(F32) + two.astype(F32)).astype(BF16)

    keep, send = on_core(
        parts_kernel, "parts", [SMEM],
        (jnp.stack([col_index, head_index]), key_value_grad, local, w_qg, w_kv),
        (((wide, C), F32), ((wide, C), BF16)), [pltpu.VMEM((keys, C), F32)],
    )
    raw = summed(raw, exchange(raw, staggered(other_row, next_col)))
    raw = summed(raw, exchange(raw, staggered(far_col, other_row)))
    parts = keep + exchange(send, other_head).astype(F32)
    parts = parts[:TILE] + exchange(parts[TILE:].astype(BF16), far_col).astype(F32)
    half = TILE // 2
    pair_grad = parts[:half] + exchange(parts[half:].astype(BF16), next_col).astype(F32)
    total, squares = on_core(
        squares_kernel, "squares", [], (raw, exchange(raw, staggered(next_col, far_col))),
        (((5 * width, C), F32), ((8, C), F32)),
    )
    grads = on_core(
        clip_kernel, "clip", [], (total, squares, exchange(squares, other_head)),
        (((width, C), F32),) * 5,
    )
    query_grad, gate_grad, key_grad, value_grad, out_weight_grad = grads
    return (
        pair_grad.astype(BF16).reshape(1, half, C),
        query_grad.T,
        key_grad.T,
        value_grad.T,
        gate_grad.T,
        out_weight_grad,
    )


def per_device(pair, out_grad, pair_bias, *rest):
    small = lax.axis_size("col") == 4 and lax.axis_size("row") == 2 and lax.axis_size("head") == 2
    if small and pair.shape == (1, TILE, C) and pair_bias.shape == (TILE, 2, 4 * TILE):
        return four_cols(pair, out_grad, pair_bias, *rest)
    return any_cols(pair, out_grad, pair_bias, *rest)


def solution(mesh):
    return jax.shard_map(
        per_device,
        mesh=mesh,
        in_specs=(
            P(("groups", "row"), "col", None),
            P(("groups", "row"), "col", None),
            P(("groups", "col"), "head", None),
            P(None, "head"),
            P(None, "head"),
            P(None, "head"),
            P(None, "head"),
            P("head", None),
            P("groups", None),
            P("groups"),
        ),
        out_specs=(
            P(("groups", "row"), ("col", "head"), None),
            P("groups", "head"),
            P("groups", "head"),
            P("groups", "head"),
            P("groups", "head"),
            P(("groups", "head"), None),
        ),
        check_vma=False,
    )
```

```python
import math

import jax
import jax.numpy as jnp
from jax import lax
from jax.experimental import pallas as pl
from jax.experimental.pallas import tpu as pltpu
from jax.sharding import PartitionSpec as P

C = 128
H = 4
HD = 32
TILE = 128


NEG_FILL = -1e30
F32 = jnp.float32
BF16 = jnp.bfloat16
CLIP_NORM = 0.5 * math.sqrt(5.0 * C * H * HD)


def shifted(value, axis, steps):
    count = lax.axis_size(axis)
    pairs = [(source, (source + steps) % count) for source in range(count)]
    return lax.ppermute(value, axis, pairs)


def allowed_between(tile_mask, chain_ids, query_start, query_count, key_start, key_count):
    tile_ids = jnp.arange(tile_mask.shape[0], dtype=jnp.int32)
    query_pos = query_start + jnp.arange(query_count, dtype=jnp.int32)
    key_pos = key_start + jnp.arange(key_count, dtype=jnp.int32)
    query_tiles = (query_pos[:, None] // TILE == tile_ids[None, :]).astype(jnp.float32)
    key_tiles = (key_pos[:, None] // TILE == tile_ids[None, :]).astype(jnp.float32)
    marks = jnp.dot(jnp.dot(query_tiles, tile_mask.astype(jnp.float32)), key_tiles.T)
    query_chain = lax.dynamic_slice_in_dim(chain_ids, query_start, query_count)
    key_chain = lax.dynamic_slice_in_dim(chain_ids, key_start, key_count)
    return (marks > 0.5) | (query_chain[:, None] == key_chain[None, :])


def score_block(query_four, key_four, bias_block, allowed):
    scores = jnp.einsum("rjhd,rkhd->rjhk", query_four, key_four, preferred_element_type=jnp.float32)
    scores = scores + bias_block[None].astype(jnp.float32)
    return jnp.where(allowed[None, :, None, :], scores, NEG_FILL)


def prob_and_grad(
    query_four, grad_four, log_total, delta_sum, key_four, value_four, bias_block, allowed
):
    scores = score_block(query_four, key_four, bias_block, allowed)
    prob = jnp.where(allowed[None, :, None, :], jnp.exp(scores - log_total[..., None]), 0.0)
    grad_prob = jnp.einsum(
        "rjhd,rkhd->rjhk", grad_four, value_four, preferred_element_type=jnp.float32
    )
    grad_score = (prob * (grad_prob - delta_sum[..., None])).astype(jnp.bfloat16)
    return (prob.astype(jnp.bfloat16), grad_score)


def any_cols(
    pair, out_grad, pair_bias, w_query, w_key, w_value, w_gate, w_out, tile_mask, chain_ids
):
    rows_dev, cols_dev, channels = pair.shape
    heads_dev = pair_bias.shape[1]
    head_width = w_query.shape[1]
    head_size = head_width // heads_dev
    hd_scale = head_size ** (-0.5)
    col_count = lax.axis_size("col")
    col_index = lax.axis_index("col")
    col_start = col_index * cols_dev
    shape_four = (rows_dev, cols_dev, heads_dev, head_size)
    stat_shape = (rows_dev, cols_dev, heads_dev)
    flat_pair = pair.reshape(rows_dev * cols_dev, channels)
    flat_grad = out_grad.reshape(rows_dev * cols_dev, channels)
    w_joined = jnp.concatenate([w_query, w_key, w_value, w_gate], axis=1)
    projected = jnp.dot(flat_pair, w_joined, preferred_element_type=jnp.float32)
    query_flat = (projected[:, :head_width] * hd_scale).astype(jnp.bfloat16)
    key_grid = (
        projected[:, head_width : 2 * head_width]
        .astype(jnp.bfloat16)
        .reshape(rows_dev, cols_dev, head_width)
    )
    value_grid = (
        projected[:, 2 * head_width : 3 * head_width]
        .astype(jnp.bfloat16)
        .reshape(rows_dev, cols_dev, head_width)
    )
    gate_value = jax.nn.sigmoid(projected[:, 3 * head_width :])
    query_four = query_flat.reshape(shape_four)
    key_piece = lax.all_gather(key_grid, "col", axis=1, tiled=True)
    value_piece = lax.all_gather(value_grid, "col", axis=1, tiled=True)
    key_count = key_piece.shape[1]
    allowed = allowed_between(tile_mask, chain_ids, col_start, cols_dev, jnp.int32(0), key_count)
    bias_block = pair_bias
    run_max = jnp.full(stat_shape, NEG_FILL, jnp.float32)
    key_four = key_piece.reshape(rows_dev, key_count, heads_dev, head_size)
    value_four = value_piece.reshape(rows_dev, key_count, heads_dev, head_size)
    scores = score_block(query_four, key_four, bias_block, allowed)
    new_max = jnp.maximum(run_max, jnp.max(scores, axis=3))
    weights = jnp.where(allowed[None, :, None, :], jnp.exp(scores - new_max[..., None]), 0.0)
    new_sum = jnp.sum(weights, axis=3)
    added = jnp.einsum(
        "rjhk,rkhd->rjhd",
        weights.astype(jnp.bfloat16),
        value_four,
        preferred_element_type=jnp.float32,
    )
    attended = (added / new_sum[..., None]).reshape(rows_dev * cols_dev, head_width)
    log_total = new_max + jnp.log(new_sum)
    gated = (gate_value * attended).astype(jnp.bfloat16)
    grad_gated = jnp.dot(flat_grad, w_out.T, preferred_element_type=jnp.float32)
    grad_att = (grad_gated * gate_value).astype(jnp.bfloat16)
    grad_gate_logit = (grad_gated * attended * gate_value * (1.0 - gate_value)).astype(jnp.bfloat16)
    delta_sum = jnp.sum((grad_att.astype(jnp.float32) * attended).reshape(shape_four), axis=3)
    grad_four = grad_att.reshape(shape_four)

    def back_turn(turn_index, loop_state):
        travel_keys, travel_grads, query_acc = loop_state
        owner_col = jnp.mod(col_index - turn_index, col_count)
        key_start = owner_col * cols_dev
        allowed = allowed_between(tile_mask, chain_ids, col_start, cols_dev, key_start, cols_dev)
        bias_block = lax.dynamic_slice_in_dim(pair_bias, key_start, cols_dev, 2)
        grads_in = travel_grads
        query_in = query_acc
        key_four = travel_keys[0].reshape(shape_four)
        value_four = travel_keys[1].reshape(shape_four)
        prob_bf, grad_score = prob_and_grad(
            query_four, grad_four, log_total, delta_sum, key_four, value_four, bias_block, allowed
        )
        query_more = jnp.einsum(
            "rjhk,rkhd->rjhd", grad_score, key_four, preferred_element_type=jnp.float32
        )
        key_more = jnp.einsum(
            "rjhk,rjhd->rkhd", grad_score, query_four, preferred_element_type=jnp.float32
        )
        value_more = jnp.einsum(
            "rjhk,rjhd->rkhd", prob_bf, grad_four, preferred_element_type=jnp.float32
        )
        travel_grads = grads_in + jnp.stack([key_more, value_more]).reshape(grads_in.shape)
        query_acc = query_in + query_more
        travel_keys = shifted(travel_keys, "col", 1)
        travel_grads = shifted(travel_grads.astype(jnp.bfloat16), "col", 1).astype(
            travel_grads.dtype
        )
        return (travel_keys, travel_grads, query_acc)

    def back_pair(pair_index, loop_state):
        for half_turn in range(2):
            loop_state = back_turn(2 * pair_index + half_turn, loop_state)
        return loop_state

    loop_start = (
        jnp.stack([key_grid, value_grid]),
        jnp.zeros((2, rows_dev, cols_dev, head_width), jnp.float32),
        jnp.zeros(shape_four, jnp.float32),
    )
    travel_keys, key_value_acc, query_acc = lax.fori_loop(0, col_count // 2, back_pair, loop_start)
    query_grad = (
        (query_acc * hd_scale).astype(jnp.bfloat16).reshape(rows_dev * cols_dev, head_width)
    )
    key_grad = key_value_acc[0].astype(jnp.bfloat16).reshape(rows_dev * cols_dev, head_width)
    value_grad = key_value_acc[1].astype(jnp.bfloat16).reshape(rows_dev * cols_dev, head_width)
    grad_joined = jnp.concatenate([query_grad, key_grad, value_grad, grad_gate_logit], axis=1)
    partial_pair = jnp.dot(grad_joined, w_joined.T, preferred_element_type=jnp.float32).reshape(
        rows_dev, cols_dev, channels
    )
    pair_grad = lax.psum_scatter(
        partial_pair.astype(jnp.bfloat16), "head", scatter_dimension=1, tiled=True
    )
    raw_four = jnp.dot(flat_pair.T, grad_joined, preferred_element_type=jnp.float32)
    raw_out = jnp.dot(gated.T, flat_grad, preferred_element_type=jnp.float32)
    summed_four, summed_out = lax.psum((raw_four, raw_out), ("col", "row"))
    local_squares = jnp.sum(summed_four * summed_four) + jnp.sum(summed_out * summed_out)
    squares = lax.psum(local_squares, "head")
    clip = jnp.minimum(1.0, 0.5 * math.sqrt(5.0 * C * H * HD) / jnp.sqrt(squares + 1e-06))
    return (
        pair_grad,
        summed_four[:, :head_width] * clip,
        summed_four[:, head_width : 2 * head_width] * clip,
        summed_four[:, 2 * head_width : 3 * head_width] * clip,
        summed_four[:, 3 * head_width :] * clip,
        summed_out * clip,
    )


def exchange(value, partner):
    cols, rows, heads = lax.axis_size("col"), lax.axis_size("row"), lax.axis_size("head")
    pairs = []
    for col in range(cols):
        for row in range(rows):
            for head in range(heads):
                to_col, to_row, to_head = partner(col, row, head)
                source = (col * rows + row) * heads + head
                pairs.append((source, (to_col * rows + to_row) * heads + to_head))
    return lax.ppermute(value, ("col", "row", "head"), pairs)


def next_col(col, row, head):
    return col ^ 1, row, head


def far_col(col, row, head):
    return col ^ 2, row, head


def end_col(col, row, head):
    return col ^ 3, row, head


def other_row(col, row, head):
    return col, row ^ 1, head


def other_head(col, row, head):
    return col, row, head ^ 1


def staggered(first, second):
    return lambda col, row, head: (first, second)[head](col, row, head)


def dot_nn(left, right):
    return jnp.dot(left, right, preferred_element_type=F32)


def dot_nt(left, right):
    return lax.dot_general(left, right, (((1,), (1,)), ((), ())), preferred_element_type=F32)


def split_rows(flat):
    first = lax.broadcasted_iota(jnp.int32, flat.shape, 0) < HD
    zero = jnp.zeros_like(flat)
    return jnp.concatenate([jnp.where(first, flat, zero), jnp.where(first, zero, flat)], axis=1)


def join_rows(wide):
    count = wide.shape[1] // 2
    first = lax.broadcasted_iota(jnp.int32, (wide.shape[0], count), 0) < HD
    return jnp.where(first, wide[:, :count], wide[:, count:])


def split_cols(flat):
    first = lax.broadcasted_iota(jnp.int32, flat.shape, 1) < HD
    zero = jnp.zeros_like(flat)
    return jnp.concatenate([jnp.where(first, flat, zero), jnp.where(first, zero, flat)], axis=0)


def local_kernel(
    col_ref, tile_hbm, x_hbm, grad_hbm, bias_hbm, chain_hbm, wq_hbm, wk_hbm, wv_hbm, wg_hbm, wo_hbm,
    x_ref, grad_ref, w_qg_ref, w_kv_ref, bias_out, left_out, right_out, gate_out, gated_grad_out,
    att_grad_out, tile_ref, chain_ref, wo_ref, bias_ref, sems,
):
    scale = HD ** (-0.5)
    width = 2 * TILE
    me = col_ref[0]
    moves = [
        (x_hbm, x_ref),
        (wq_hbm, w_qg_ref.at[: 2 * HD]),
        (wg_hbm, w_qg_ref.at[2 * HD :]),
        (grad_hbm, grad_ref),
        (wo_hbm, wo_ref),
        (chain_hbm, chain_ref),
        (tile_hbm, tile_ref),
        (bias_hbm, bias_ref),
        (wk_hbm, w_kv_ref.at[: 2 * HD]),
        (wv_hbm, w_kv_ref.at[2 * HD :]),
    ]
    copies = [
        pltpu.make_async_copy(source, target, sems.at[place])
        for place, (source, target) in enumerate(moves)
    ]
    for copy in copies:
        copy.start()
    for copy in copies[:5]:
        copy.wait()
    x = x_ref[...]
    query_gate = dot_nt(w_qg_ref[...], x)
    gated_grad_t = dot_nt(wo_ref[...], grad_ref[...])
    query = (dot_nt(x, w_qg_ref[: 2 * HD, :]) * scale).astype(BF16)
    query_t = (query_gate[: 2 * HD] * scale).astype(BF16)
    gate_t = jax.nn.sigmoid(query_gate[2 * HD :])
    att_grad_t = (gated_grad_t * gate_t).astype(BF16)
    att_grad_f = att_grad_t.astype(F32)
    att_grad = jnp.transpose(att_grad_f).astype(BF16)
    zero_wide = jnp.zeros((2 * HD, width), BF16)
    zero_tall = jnp.zeros((width, 2 * HD), BF16)
    left_out[: 2 * HD, :] = jnp.concatenate([split_rows(query_t), zero_wide], axis=1)
    left_out[2 * HD :, :] = jnp.concatenate([zero_wide, split_rows(att_grad_t)], axis=1)
    right_out[:width, :] = jnp.concatenate([split_cols(query), zero_tall], axis=1)
    right_out[width:, :] = jnp.concatenate([zero_tall, split_cols(att_grad)], axis=1)
    gate_out[...] = gate_t
    gated_grad_out[...] = gated_grad_t
    att_grad_out[...] = att_grad_f
    for copy in copies[5:]:
        copy.wait()
    chains = chain_ref[...].astype(F32)
    own_chain = chain_ref[pl.ds(me, 1), :].astype(F32)
    for block in range(4):
        rows = slice(block * TILE, (block + 1) * TILE)
        key_chain = jnp.transpose(jnp.broadcast_to(chains[block : block + 1, :], (TILE, TILE)))
        apart = jnp.where(tile_ref[me, block] == 1, 0.0, 1.0)
        banned = jnp.where(key_chain == own_chain, 0.0, apart) > 0.5
        for head in range(2):
            bias = bias_ref[:, head, rows].astype(F32)
            bias_out[rows, head * TILE : (head + 1) * TILE] = jnp.where(
                banned, NEG_FILL, jnp.transpose(bias)
            )


def attention_kernel(
    col_ref, head_ref, x_ref, next_ref, direct_ref, crossed_ref, grad_ref, bias_ref, left_ref, right_ref,
    gate_ref, gated_grad_ref, att_grad_ref, w_kv_ref,
    raw_ref, local_ref, key_value_grad_ref,
    pairs_ref, scores_ref, expo_ref, both_ref,
):
    scale = HD ** (-0.5)
    width = 2 * TILE
    me, head = col_ref[0], head_ref[0]
    for bits, ref in ((0, x_ref), (1, next_ref), (2 + head, direct_ref), (3 - head, crossed_ref)):
        place = pl.multiple_of(lax.bitwise_xor(me, bits) * TILE, TILE)
        pairs_ref[pl.ds(place, TILE), :] = ref[...]
    w_kv = w_kv_ref[...]
    pairs = pairs_ref[...]
    key_value = dot_nt(pairs, w_kv).astype(BF16)
    key_value_t = dot_nt(w_kv, pairs).astype(BF16)
    left = left_ref[...]
    top = None
    for block in range(4):
        rows = slice(block * TILE, (block + 1) * TILE)
        product = dot_nn(key_value[rows], left)
        scores = product[:, :width] + bias_ref[rows, :]
        scores_ref[rows, :width] = scores
        scores_ref[rows, width:] = product[:, width:]
        part = jnp.max(scores.reshape(TILE // 8, 8, width), axis=0)
        top = part if top is None else jnp.maximum(top, part)
    top = jnp.max(top, axis=0, keepdims=True)
    total = jnp.zeros((8, width), F32)
    for block in range(4):
        rows = slice(block * TILE, (block + 1) * TILE)
        expo = jnp.exp(scores_ref[rows, :width] - top)
        scores_ref[rows, :width] = expo
        expo_ref[rows, :] = expo.astype(BF16)
        total = total + jnp.sum(expo.reshape(TILE // 8, 8, width), axis=0)
    inverse = 1.0 / jnp.sum(total, axis=0, keepdims=True)
    attended_t = join_rows(dot_nn(key_value_t[2 * HD :], expo_ref[...]) * inverse)
    gate_t, gated_grad_t = gate_ref[...], gated_grad_ref[...]
    gated_t = (gate_t * attended_t).astype(BF16)
    gate_logit_t = gated_grad_t * attended_t * gate_t * (1.0 - gate_t)
    products = att_grad_ref[...] * attended_t
    delta = jnp.concatenate(
        [
            jnp.sum(products[:HD], axis=0, keepdims=True),
            jnp.sum(products[HD:], axis=0, keepdims=True),
        ],
        axis=1,
    )
    for block in range(4):
        rows = slice(block * TILE, (block + 1) * TILE)
        prob = scores_ref[rows, :width] * inverse
        both_ref[rows, :width] = (prob * (scores_ref[rows, width:] - delta)).astype(BF16)
        both_ref[rows, width:] = prob.astype(BF16)
    query_grad_t = join_rows(dot_nn(key_value_t[: 2 * HD], both_ref[:, :width])) * scale
    key_value_grad = dot_nn(both_ref[...], right_ref[...])
    local_t = jnp.concatenate([query_grad_t, gate_logit_t], axis=0)
    local_ref[...] = jnp.transpose(local_t).astype(BF16)
    key_value_grad_ref[...] = key_value_grad.astype(BF16)
    raw_ref[: 4 * HD, :] = dot_nn(local_t.astype(BF16), x_ref[...]).astype(BF16)
    raw_ref[4 * HD : 8 * HD, :] = dot_nn(jnp.transpose(key_value_grad).astype(BF16), pairs).astype(BF16)
    raw_ref[8 * HD :, :] = dot_nn(gated_t, grad_ref[...]).astype(BF16)


def parts_kernel(
    col_ref, head_ref, key_value_grad_ref, local_ref, w_qg_ref, w_kv_ref, keep_ref, send_ref, parts_ref
):
    me, head = col_ref[0], head_ref[0]
    half = TILE // 2
    parts_ref[...] = dot_nn(key_value_grad_ref[...], w_kv_ref[...])
    own = pl.ds(pl.multiple_of(me * TILE, TILE), TILE)
    parts_ref[own, :] = parts_ref[own, :] + dot_nn(local_ref[...], w_qg_ref[...])
    for bits in range(4):
        start = lax.bitwise_xor(me, bits) * TILE
        mine = pl.multiple_of(start + head * half, half)
        other = pl.multiple_of(start + (1 - head) * half, half)
        rows = slice(bits * half, (bits + 1) * half)
        keep_ref[rows, :] = parts_ref[pl.ds(mine, half), :]
        send_ref[rows, :] = parts_ref[pl.ds(other, half), :].astype(BF16)


def squares_kernel(own_ref, other_ref, total_ref, squares_ref):
    total = own_ref[...].astype(F32) + other_ref[...].astype(F32)
    total_ref[...] = total
    squares_ref[...] = jnp.sum((total * total).reshape(total.shape[0] // 8, 8, C), axis=0)


def clip_kernel(total_ref, own_ref, other_ref, query_ref, gate_ref, key_ref, value_ref, out_ref):
    squares = own_ref[...] + other_ref[...]
    squares = jnp.sum(jnp.sum(squares, axis=0, keepdims=True), axis=1, keepdims=True)
    clip = jnp.minimum(1.0, CLIP_NORM / jnp.sqrt(squares + 1e-06))
    for part, ref in enumerate((query_ref, gate_ref, key_ref, value_ref, out_ref)):
        ref[...] = total_ref[part * 2 * HD : (part + 1) * 2 * HD, :] * clip


VMEM = pl.BlockSpec(memory_space=pltpu.VMEM)
SMEM = pl.BlockSpec(memory_space=pltpu.SMEM)
HBM = pl.BlockSpec(memory_space=pltpu.HBM)


def on_core(kernel, name, specs, operands, outs, scratch=(), cost=1 << 18):
    return pl.pallas_call(
        kernel,
        out_shape=tuple(jax.ShapeDtypeStruct(shape, dtype) for shape, dtype in outs),
        in_specs=specs + [VMEM] * (len(operands) - len(specs)),
        out_specs=(VMEM,) * len(outs),
        scratch_shapes=scratch,
        compiler_params=pltpu.CompilerParams(vmem_limit_bytes=16 << 20),
        cost_estimate=pl.CostEstimate(flops=1 << 20, bytes_accessed=cost, transcendentals=0),
        name=name,
    )(
        *(
            pltpu.with_memory_space_constraint(operand, pltpu.HBM) if spec is HBM else operand
            for spec, operand in zip(specs + [VMEM] * len(operands), operands)
        )
    )


def four_cols(
    pair, out_grad, pair_bias, w_query, w_key, w_value, w_gate, w_out, tile_mask, chain_ids
):
    col_index = lax.axis_index("col")
    head_index = lax.axis_index("head")
    col = col_index.reshape(1)
    width, keys, wide = 2 * HD, 4 * TILE, 2 * TILE
    x = pair.reshape(TILE, C)
    head = head_index.reshape(1)
    x_direct = exchange(x, staggered(far_col, end_col))
    x_next = exchange(x, next_col)
    x, grad, w_qg, w_kv, bias, left, right, gate_t, gated_grad_t, att_grad_t = on_core(
        local_kernel, "local", [SMEM] + [HBM] * 10,
        (
            col, tile_mask, x, out_grad.reshape(TILE, C), pair_bias, chain_ids.reshape(4, TILE),
            w_query.T, w_key.T, w_value.T, w_gate.T, w_out,
        ),
        (
            ((TILE, C), BF16), ((TILE, C), BF16), ((2 * width, C), BF16), ((2 * width, C), BF16),
            ((keys, wide), F32), ((C, 2 * wide), BF16), ((2 * wide, C), BF16),
            ((width, TILE), F32), ((width, TILE), F32), ((width, TILE), F32),
        ),
        [
            pltpu.SMEM((4, 4), jnp.int32), pltpu.VMEM((4, TILE), jnp.int32),
            pltpu.VMEM((width, C), BF16), pltpu.VMEM((TILE, 2, keys), BF16),
            pltpu.SemaphoreType.DMA((10,)),
        ],
    )
    x_direct, w_kv = lax.optimization_barrier((x_direct, w_kv))
    x_crossed = exchange(x_direct, other_head)
    raw, local, key_value_grad = on_core(
        attention_kernel, "attention", [SMEM, SMEM],
        (col, head, x, x_next, x_direct, x_crossed, grad, bias, left, right, gate_t, gated_grad_t, att_grad_t, w_kv),
        (((5 * width, C), BF16), ((TILE, C), BF16), ((keys, C), BF16)),
        [
            pltpu.VMEM((keys, C), BF16), pltpu.VMEM((keys, 2 * wide), F32),
            pltpu.VMEM((keys, wide), BF16), pltpu.VMEM((keys, 2 * wide), BF16),
        ],
    )

    def summed(one, two):
        return (one.astype(F32) + two.astype(F32)).astype(BF16)

    keep, send = on_core(
        parts_kernel, "parts", [SMEM, SMEM], (col, head, key_value_grad, local, w_qg, w_kv),
        (((wide, C), F32), ((wide, C), BF16)), [pltpu.VMEM((keys, C), F32)],
    )
    half = TILE // 2
    raw = summed(raw, exchange(raw, staggered(other_row, next_col)))
    parts = keep + exchange(send, other_head).astype(F32)
    kept, sent = parts[:TILE], parts[TILE:].astype(BF16)
    raw, kept = lax.optimization_barrier((raw, kept))
    parts = kept + exchange(sent, far_col).astype(F32)
    raw = summed(raw, exchange(raw, staggered(far_col, other_row)))
    kept, sent = parts[:half], parts[half:].astype(BF16)
    raw, kept = lax.optimization_barrier((raw, kept))
    pair_grad = (kept + exchange(sent, next_col).astype(F32)).astype(BF16)
    last = exchange(raw, staggered(next_col, far_col))
    last, pair_grad = lax.optimization_barrier((last, pair_grad))
    total, squares = on_core(
        squares_kernel, "squares", [], (raw, last), (((5 * width, C), F32), ((8, C), F32)),
    )
    grads = on_core(
        clip_kernel, "clip", [], (total, squares, exchange(squares, other_head)),
        (((width, C), F32),) * 5,
    )
    query_grad, gate_grad, key_grad, value_grad, out_weight_grad = grads
    return (
        pair_grad.reshape(1, half, C),
        query_grad.T,
        key_grad.T,
        value_grad.T,
        gate_grad.T,
        out_weight_grad,
    )


def per_device(pair, out_grad, pair_bias, *rest):
    small = lax.axis_size("col") == 4 and lax.axis_size("row") == 2 and lax.axis_size("head") == 2
    if small and pair.shape == (1, TILE, C) and pair_bias.shape == (TILE, 2, 4 * TILE):
        return four_cols(pair, out_grad, pair_bias, *rest)
    return any_cols(pair, out_grad, pair_bias, *rest)


def solution(mesh):
    return jax.shard_map(
        per_device,
        mesh=mesh,
        in_specs=(
            P(("groups", "row"), "col", None),
            P(("groups", "row"), "col", None),
            P(("groups", "col"), "head", None),
            P(None, "head"),
            P(None, "head"),
            P(None, "head"),
            P(None, "head"),
            P("head", None),
            P("groups", None),
            P("groups"),
        ),
        out_specs=(
            P(("groups", "row"), ("col", "head"), None),
            P("groups", "head"),
            P("groups", "head"),
            P("groups", "head"),
            P("groups", "head"),
            P(("groups", "head"), None),
        ),
        check_vma=False,
    )
```

```python
import math

import jax
import jax.numpy as jnp
from jax import lax
from jax.experimental import pallas as pl
from jax.experimental.pallas import tpu as pltpu
from jax.sharding import PartitionSpec as P

C = 128
H = 4
HD = 32
TILE = 128


NEG_FILL = -1e30
F32 = jnp.float32
BF16 = jnp.bfloat16
CLIP_NORM = 0.5 * math.sqrt(5.0 * C * H * HD)


def shifted(value, axis, steps):
    count = lax.axis_size(axis)
    pairs = [(source, (source + steps) % count) for source in range(count)]
    return lax.ppermute(value, axis, pairs)


def allowed_between(tile_mask, chain_ids, query_start, query_count, key_start, key_count):
    tile_ids = jnp.arange(tile_mask.shape[0], dtype=jnp.int32)
    query_pos = query_start + jnp.arange(query_count, dtype=jnp.int32)
    key_pos = key_start + jnp.arange(key_count, dtype=jnp.int32)
    query_tiles = (query_pos[:, None] // TILE == tile_ids[None, :]).astype(jnp.float32)
    key_tiles = (key_pos[:, None] // TILE == tile_ids[None, :]).astype(jnp.float32)
    marks = jnp.dot(jnp.dot(query_tiles, tile_mask.astype(jnp.float32)), key_tiles.T)
    query_chain = lax.dynamic_slice_in_dim(chain_ids, query_start, query_count)
    key_chain = lax.dynamic_slice_in_dim(chain_ids, key_start, key_count)
    return (marks > 0.5) | (query_chain[:, None] == key_chain[None, :])


def score_block(query_four, key_four, bias_block, allowed):
    scores = jnp.einsum("rjhd,rkhd->rjhk", query_four, key_four, preferred_element_type=jnp.float32)
    scores = scores + bias_block[None].astype(jnp.float32)
    return jnp.where(allowed[None, :, None, :], scores, NEG_FILL)


def prob_and_grad(
    query_four, grad_four, log_total, delta_sum, key_four, value_four, bias_block, allowed
):
    scores = score_block(query_four, key_four, bias_block, allowed)
    prob = jnp.where(allowed[None, :, None, :], jnp.exp(scores - log_total[..., None]), 0.0)
    grad_prob = jnp.einsum(
        "rjhd,rkhd->rjhk", grad_four, value_four, preferred_element_type=jnp.float32
    )
    grad_score = (prob * (grad_prob - delta_sum[..., None])).astype(jnp.bfloat16)
    return (prob.astype(jnp.bfloat16), grad_score)


def any_cols(
    pair, out_grad, pair_bias, w_query, w_key, w_value, w_gate, w_out, tile_mask, chain_ids
):
    rows_dev, cols_dev, channels = pair.shape
    heads_dev = pair_bias.shape[1]
    head_width = w_query.shape[1]
    head_size = head_width // heads_dev
    hd_scale = head_size ** (-0.5)
    col_count = lax.axis_size("col")
    col_index = lax.axis_index("col")
    col_start = col_index * cols_dev
    shape_four = (rows_dev, cols_dev, heads_dev, head_size)
    stat_shape = (rows_dev, cols_dev, heads_dev)
    flat_pair = pair.reshape(rows_dev * cols_dev, channels)
    flat_grad = out_grad.reshape(rows_dev * cols_dev, channels)
    w_joined = jnp.concatenate([w_query, w_key, w_value, w_gate], axis=1)
    projected = jnp.dot(flat_pair, w_joined, preferred_element_type=jnp.float32)
    query_flat = (projected[:, :head_width] * hd_scale).astype(jnp.bfloat16)
    key_grid = (
        projected[:, head_width : 2 * head_width]
        .astype(jnp.bfloat16)
        .reshape(rows_dev, cols_dev, head_width)
    )
    value_grid = (
        projected[:, 2 * head_width : 3 * head_width]
        .astype(jnp.bfloat16)
        .reshape(rows_dev, cols_dev, head_width)
    )
    gate_value = jax.nn.sigmoid(projected[:, 3 * head_width :])
    query_four = query_flat.reshape(shape_four)
    key_piece = lax.all_gather(key_grid, "col", axis=1, tiled=True)
    value_piece = lax.all_gather(value_grid, "col", axis=1, tiled=True)
    key_count = key_piece.shape[1]
    allowed = allowed_between(tile_mask, chain_ids, col_start, cols_dev, jnp.int32(0), key_count)
    bias_block = pair_bias
    run_max = jnp.full(stat_shape, NEG_FILL, jnp.float32)
    key_four = key_piece.reshape(rows_dev, key_count, heads_dev, head_size)
    value_four = value_piece.reshape(rows_dev, key_count, heads_dev, head_size)
    scores = score_block(query_four, key_four, bias_block, allowed)
    new_max = jnp.maximum(run_max, jnp.max(scores, axis=3))
    weights = jnp.where(allowed[None, :, None, :], jnp.exp(scores - new_max[..., None]), 0.0)
    new_sum = jnp.sum(weights, axis=3)
    added = jnp.einsum(
        "rjhk,rkhd->rjhd",
        weights.astype(jnp.bfloat16),
        value_four,
        preferred_element_type=jnp.float32,
    )
    attended = (added / new_sum[..., None]).reshape(rows_dev * cols_dev, head_width)
    log_total = new_max + jnp.log(new_sum)
    gated = (gate_value * attended).astype(jnp.bfloat16)
    grad_gated = jnp.dot(flat_grad, w_out.T, preferred_element_type=jnp.float32)
    grad_att = (grad_gated * gate_value).astype(jnp.bfloat16)
    grad_gate_logit = (grad_gated * attended * gate_value * (1.0 - gate_value)).astype(jnp.bfloat16)
    delta_sum = jnp.sum((grad_att.astype(jnp.float32) * attended).reshape(shape_four), axis=3)
    grad_four = grad_att.reshape(shape_four)

    def back_turn(turn_index, loop_state):
        travel_keys, travel_grads, query_acc = loop_state
        owner_col = jnp.mod(col_index - turn_index, col_count)
        key_start = owner_col * cols_dev
        allowed = allowed_between(tile_mask, chain_ids, col_start, cols_dev, key_start, cols_dev)
        bias_block = lax.dynamic_slice_in_dim(pair_bias, key_start, cols_dev, 2)
        grads_in = travel_grads
        query_in = query_acc
        key_four = travel_keys[0].reshape(shape_four)
        value_four = travel_keys[1].reshape(shape_four)
        prob_bf, grad_score = prob_and_grad(
            query_four, grad_four, log_total, delta_sum, key_four, value_four, bias_block, allowed
        )
        query_more = jnp.einsum(
            "rjhk,rkhd->rjhd", grad_score, key_four, preferred_element_type=jnp.float32
        )
        key_more = jnp.einsum(
            "rjhk,rjhd->rkhd", grad_score, query_four, preferred_element_type=jnp.float32
        )
        value_more = jnp.einsum(
            "rjhk,rjhd->rkhd", prob_bf, grad_four, preferred_element_type=jnp.float32
        )
        travel_grads = grads_in + jnp.stack([key_more, value_more]).reshape(grads_in.shape)
        query_acc = query_in + query_more
        travel_keys = shifted(travel_keys, "col", 1)
        travel_grads = shifted(travel_grads.astype(jnp.bfloat16), "col", 1).astype(
            travel_grads.dtype
        )
        return (travel_keys, travel_grads, query_acc)

    def back_pair(pair_index, loop_state):
        for half_turn in range(2):
            loop_state = back_turn(2 * pair_index + half_turn, loop_state)
        return loop_state

    loop_start = (
        jnp.stack([key_grid, value_grid]),
        jnp.zeros((2, rows_dev, cols_dev, head_width), jnp.float32),
        jnp.zeros(shape_four, jnp.float32),
    )
    travel_keys, key_value_acc, query_acc = lax.fori_loop(0, col_count // 2, back_pair, loop_start)
    query_grad = (
        (query_acc * hd_scale).astype(jnp.bfloat16).reshape(rows_dev * cols_dev, head_width)
    )
    key_grad = key_value_acc[0].astype(jnp.bfloat16).reshape(rows_dev * cols_dev, head_width)
    value_grad = key_value_acc[1].astype(jnp.bfloat16).reshape(rows_dev * cols_dev, head_width)
    grad_joined = jnp.concatenate([query_grad, key_grad, value_grad, grad_gate_logit], axis=1)
    partial_pair = jnp.dot(grad_joined, w_joined.T, preferred_element_type=jnp.float32).reshape(
        rows_dev, cols_dev, channels
    )
    pair_grad = lax.psum_scatter(
        partial_pair.astype(jnp.bfloat16), "head", scatter_dimension=1, tiled=True
    )
    raw_four = jnp.dot(flat_pair.T, grad_joined, preferred_element_type=jnp.float32)
    raw_out = jnp.dot(gated.T, flat_grad, preferred_element_type=jnp.float32)
    summed_four, summed_out = lax.psum((raw_four, raw_out), ("col", "row"))
    local_squares = jnp.sum(summed_four * summed_four) + jnp.sum(summed_out * summed_out)
    squares = lax.psum(local_squares, "head")
    clip = jnp.minimum(1.0, 0.5 * math.sqrt(5.0 * C * H * HD) / jnp.sqrt(squares + 1e-06))
    return (
        pair_grad,
        summed_four[:, :head_width] * clip,
        summed_four[:, head_width : 2 * head_width] * clip,
        summed_four[:, 2 * head_width : 3 * head_width] * clip,
        summed_four[:, 3 * head_width :] * clip,
        summed_out * clip,
    )


def exchange(value, partner):
    cols, rows, heads = lax.axis_size("col"), lax.axis_size("row"), lax.axis_size("head")
    pairs = []
    for col in range(cols):
        for row in range(rows):
            for head in range(heads):
                to_col, to_row, to_head = partner(col, row, head)
                source = (col * rows + row) * heads + head
                pairs.append((source, (to_col * rows + to_row) * heads + to_head))
    return lax.ppermute(value, ("col", "row", "head"), pairs)


def next_col(col, row, head):
    return col ^ 1, row, head


def far_col(col, row, head):
    return col ^ 2, row, head


def end_col(col, row, head):
    return col ^ 3, row, head


def other_row(col, row, head):
    return col, row ^ 1, head


def other_head(col, row, head):
    return col, row, head ^ 1


def staggered(first, second):
    return lambda col, row, head: (first, second)[head](col, row, head)


def dot_nn(left, right):
    return jnp.dot(left, right, preferred_element_type=F32)


def dot_nt(left, right):
    return lax.dot_general(left, right, (((1,), (1,)), ((), ())), preferred_element_type=F32)


def split_rows(flat):
    first = lax.broadcasted_iota(jnp.int32, flat.shape, 0) < HD
    zero = jnp.zeros_like(flat)
    return jnp.concatenate([jnp.where(first, flat, zero), jnp.where(first, zero, flat)], axis=1)


def join_rows(wide):
    count = wide.shape[1] // 2
    first = lax.broadcasted_iota(jnp.int32, (wide.shape[0], count), 0) < HD
    return jnp.where(first, wide[:, :count], wide[:, count:])


def split_cols(flat):
    first = lax.broadcasted_iota(jnp.int32, flat.shape, 1) < HD
    zero = jnp.zeros_like(flat)
    return jnp.concatenate([jnp.where(first, flat, zero), jnp.where(first, zero, flat)], axis=0)


def local_kernel(
    col_ref, tile_hbm, x_hbm, grad_hbm, bias_hbm, chain_hbm, wq_hbm, wk_hbm, wv_hbm, wg_hbm, wo_hbm,
    x_ref, grad_ref, w_qg_ref, w_kv_ref, bias_out, left_out, right_out, gate_out, gated_grad_out,
    att_grad_out, tile_ref, chain_ref, wo_ref, bias_ref, sems,
):
    scale = HD ** (-0.5)
    width = 2 * TILE
    me = col_ref[0]
    moves = [
        (x_hbm, x_ref),
        (wq_hbm, w_qg_ref.at[: 2 * HD]),
        (wg_hbm, w_qg_ref.at[2 * HD :]),
        (grad_hbm, grad_ref),
        (wo_hbm, wo_ref),
        (chain_hbm, chain_ref),
        (tile_hbm, tile_ref),
        (bias_hbm, bias_ref),
        (wk_hbm, w_kv_ref.at[: 2 * HD]),
        (wv_hbm, w_kv_ref.at[2 * HD :]),
    ]
    copies = [
        pltpu.make_async_copy(source, target, sems.at[place])
        for place, (source, target) in enumerate(moves)
    ]
    for copy in copies:
        copy.start()
    for copy in copies[:5]:
        copy.wait()
    x = x_ref[...]
    query_gate = dot_nt(w_qg_ref[...], x)
    gated_grad_t = dot_nt(wo_ref[...], grad_ref[...])
    query = (dot_nt(x, w_qg_ref[: 2 * HD, :]) * scale).astype(BF16)
    query_t = (query_gate[: 2 * HD] * scale).astype(BF16)
    gate_t = jax.nn.sigmoid(query_gate[2 * HD :])
    att_grad_t = (gated_grad_t * gate_t).astype(BF16)
    att_grad_f = att_grad_t.astype(F32)
    att_grad = jnp.transpose(att_grad_f).astype(BF16)
    zero_wide = jnp.zeros((2 * HD, width), BF16)
    zero_tall = jnp.zeros((width, 2 * HD), BF16)
    left_out[: 2 * HD, :] = jnp.concatenate([split_rows(query_t), zero_wide], axis=1)
    left_out[2 * HD :, :] = jnp.concatenate([zero_wide, split_rows(att_grad_t)], axis=1)
    right_out[:width, :] = jnp.concatenate([split_cols(query), zero_tall], axis=1)
    right_out[width:, :] = jnp.concatenate([zero_tall, split_cols(att_grad)], axis=1)
    gate_out[...] = gate_t
    gated_grad_out[...] = gated_grad_t
    att_grad_out[...] = att_grad_f
    for copy in copies[5:]:
        copy.wait()
    chains = chain_ref[...].astype(F32)
    own_chain = chain_ref[pl.ds(me, 1), :].astype(F32)
    for block in range(4):
        rows = slice(block * TILE, (block + 1) * TILE)
        key_chain = jnp.transpose(jnp.broadcast_to(chains[block : block + 1, :], (TILE, TILE)))
        apart = jnp.where(tile_ref[me, block] == 1, 0.0, 1.0)
        banned = jnp.where(key_chain == own_chain, 0.0, apart) > 0.5
        for head in range(2):
            bias = bias_ref[:, head, rows].astype(F32)
            bias_out[rows, head * TILE : (head + 1) * TILE] = jnp.where(
                banned, NEG_FILL, jnp.transpose(bias)
            )


def attention_kernel(
    col_ref, head_ref, x_ref, next_ref, direct_ref, crossed_ref, grad_ref, bias_ref, left_ref, right_ref,
    gate_ref, gated_grad_ref, att_grad_ref, w_kv_ref,
    raw_ref, local_ref, key_value_grad_ref,
    pairs_ref, scores_ref, expo_ref, both_ref,
):
    scale = HD ** (-0.5)
    width = 2 * TILE
    me, head = col_ref[0], head_ref[0]
    for bits, ref in ((0, x_ref), (1, next_ref), (2 + head, direct_ref), (3 - head, crossed_ref)):
        place = pl.multiple_of(lax.bitwise_xor(me, bits) * TILE, TILE)
        pairs_ref[pl.ds(place, TILE), :] = ref[...]
    w_kv = w_kv_ref[...]
    pairs = pairs_ref[...]
    key_value = dot_nt(pairs, w_kv).astype(BF16)
    key_value_t = dot_nt(w_kv, pairs).astype(BF16)
    left = left_ref[...]
    top = None
    for block in range(4):
        rows = slice(block * TILE, (block + 1) * TILE)
        product = dot_nn(key_value[rows], left)
        scores = product[:, :width] + bias_ref[rows, :]
        scores_ref[rows, :width] = scores
        scores_ref[rows, width:] = product[:, width:]
        part = jnp.max(scores.reshape(TILE // 8, 8, width), axis=0)
        top = part if top is None else jnp.maximum(top, part)
    top = jnp.max(top, axis=0, keepdims=True)
    total = jnp.zeros((8, width), F32)
    for block in range(4):
        rows = slice(block * TILE, (block + 1) * TILE)
        expo = jnp.exp(scores_ref[rows, :width] - top)
        scores_ref[rows, :width] = expo
        expo_ref[rows, :] = expo.astype(BF16)
        total = total + jnp.sum(expo.reshape(TILE // 8, 8, width), axis=0)
    inverse = 1.0 / jnp.sum(total, axis=0, keepdims=True)
    attended_t = join_rows(dot_nn(key_value_t[2 * HD :], expo_ref[...]) * inverse)
    gate_t, gated_grad_t = gate_ref[...], gated_grad_ref[...]
    gated_t = (gate_t * attended_t).astype(BF16)
    gate_logit_t = gated_grad_t * attended_t * gate_t * (1.0 - gate_t)
    products = att_grad_ref[...] * attended_t
    delta = jnp.concatenate(
        [
            jnp.sum(products[:HD], axis=0, keepdims=True),
            jnp.sum(products[HD:], axis=0, keepdims=True),
        ],
        axis=1,
    )
    for block in range(4):
        rows = slice(block * TILE, (block + 1) * TILE)
        prob = scores_ref[rows, :width] * inverse
        both_ref[rows, :width] = (prob * (scores_ref[rows, width:] - delta)).astype(BF16)
        both_ref[rows, width:] = prob.astype(BF16)
    query_grad_t = join_rows(dot_nn(key_value_t[: 2 * HD], both_ref[:, :width])) * scale
    key_value_grad = dot_nn(both_ref[...], right_ref[...])
    local_t = jnp.concatenate([query_grad_t, gate_logit_t], axis=0)
    local_ref[...] = jnp.transpose(local_t).astype(BF16)
    key_value_grad_ref[...] = key_value_grad.astype(BF16)
    raw_ref[: 4 * HD, :] = dot_nn(local_t.astype(BF16), x_ref[...]).astype(BF16)
    raw_ref[4 * HD : 8 * HD, :] = dot_nn(jnp.transpose(key_value_grad).astype(BF16), pairs).astype(BF16)
    raw_ref[8 * HD :, :] = dot_nn(gated_t, grad_ref[...]).astype(BF16)


def parts_kernel(
    col_ref, head_ref, key_value_grad_ref, local_ref, w_qg_ref, w_kv_ref, keep_ref, send_ref, parts_ref
):
    me, head = col_ref[0], head_ref[0]
    half = TILE // 2
    parts_ref[...] = dot_nn(key_value_grad_ref[...], w_kv_ref[...])
    own = pl.ds(pl.multiple_of(me * TILE, TILE), TILE)
    parts_ref[own, :] = parts_ref[own, :] + dot_nn(local_ref[...], w_qg_ref[...])
    for place, bits in enumerate((0, 2, 1, 3)):
        start = lax.bitwise_xor(me, bits) * TILE
        mine = pl.multiple_of(start + head * half, half)
        other = pl.multiple_of(start + (1 - head) * half, half)
        rows = slice(place * half, (place + 1) * half)
        keep_ref[rows, :] = parts_ref[pl.ds(mine, half), :]
        send_ref[rows, :] = parts_ref[pl.ds(other, half), :].astype(BF16)


def fold_kernel(own_ref, other_ref, keep_ref, send_ref):
    half = keep_ref.shape[0]
    keep_ref[...] = own_ref[:half, :] + other_ref[:half, :].astype(F32)
    send_ref[...] = (own_ref[half:, :] + other_ref[half:, :].astype(F32)).astype(BF16)


def add_kernel(own_ref, other_ref, send_ref):
    half = send_ref.shape[0]
    send_ref[...] = (own_ref[half:, :] + other_ref[half:, :].astype(F32)).astype(BF16)


def squares_kernel(own_ref, other_ref, total_ref, squares_ref):
    total = own_ref[...].astype(F32) + other_ref[...].astype(F32)
    total_ref[...] = total
    squares_ref[...] = jnp.sum((total * total).reshape(total.shape[0] // 8, 8, C), axis=0)


def clip_kernel(
    total_ref, own_ref, other_ref, pair_own_ref, pair_other_ref,
    query_ref, gate_ref, key_ref, value_ref, out_ref, pair_ref,
):
    squares = own_ref[...] + other_ref[...]
    squares = jnp.sum(jnp.sum(squares, axis=0, keepdims=True), axis=1, keepdims=True)
    clip = jnp.minimum(1.0, CLIP_NORM / jnp.sqrt(squares + 1e-06))
    for part, ref in enumerate((query_ref, gate_ref, key_ref, value_ref, out_ref)):
        ref[...] = total_ref[part * 2 * HD : (part + 1) * 2 * HD, :] * clip
    pair_ref[...] = (pair_own_ref[...] + pair_other_ref[...].astype(F32)).astype(BF16)


VMEM = pl.BlockSpec(memory_space=pltpu.VMEM)
SMEM = pl.BlockSpec(memory_space=pltpu.SMEM)
HBM = pl.BlockSpec(memory_space=pltpu.HBM)


def on_core(kernel, name, specs, operands, outs, scratch=(), cost=1 << 18):
    return pl.pallas_call(
        kernel,
        out_shape=tuple(jax.ShapeDtypeStruct(shape, dtype) for shape, dtype in outs),
        in_specs=specs + [VMEM] * (len(operands) - len(specs)),
        out_specs=(VMEM,) * len(outs),
        scratch_shapes=scratch,
        compiler_params=pltpu.CompilerParams(vmem_limit_bytes=16 << 20),
        cost_estimate=pl.CostEstimate(flops=1 << 20, bytes_accessed=cost, transcendentals=0),
        name=name,
    )(
        *(
            pltpu.with_memory_space_constraint(operand, pltpu.HBM) if spec is HBM else operand
            for spec, operand in zip(specs + [VMEM] * len(operands), operands)
        )
    )


def four_cols(
    pair, out_grad, pair_bias, w_query, w_key, w_value, w_gate, w_out, tile_mask, chain_ids
):
    col_index = lax.axis_index("col")
    head_index = lax.axis_index("head")
    col = col_index.reshape(1)
    width, keys, wide = 2 * HD, 4 * TILE, 2 * TILE
    x = pair.reshape(TILE, C)
    head = head_index.reshape(1)
    x_direct = exchange(x, staggered(far_col, end_col))
    x_next = exchange(x, next_col)
    x, grad, w_qg, w_kv, bias, left, right, gate_t, gated_grad_t, att_grad_t = on_core(
        local_kernel, "local", [SMEM] + [HBM] * 10,
        (
            col, tile_mask, x, out_grad.reshape(TILE, C), pair_bias, chain_ids.reshape(4, TILE),
            w_query.T, w_key.T, w_value.T, w_gate.T, w_out,
        ),
        (
            ((TILE, C), BF16), ((TILE, C), BF16), ((2 * width, C), BF16), ((2 * width, C), BF16),
            ((keys, wide), F32), ((C, 2 * wide), BF16), ((2 * wide, C), BF16),
            ((width, TILE), F32), ((width, TILE), F32), ((width, TILE), F32),
        ),
        [
            pltpu.SMEM((4, 4), jnp.int32), pltpu.VMEM((4, TILE), jnp.int32),
            pltpu.VMEM((width, C), BF16), pltpu.VMEM((TILE, 2, keys), BF16),
            pltpu.SemaphoreType.DMA((10,)),
        ],
    )
    x_direct, w_kv = lax.optimization_barrier((x_direct, w_kv))
    x_crossed = exchange(x_direct, other_head)
    raw, local, key_value_grad = on_core(
        attention_kernel, "attention", [SMEM, SMEM],
        (col, head, x, x_next, x_direct, x_crossed, grad, bias, left, right, gate_t, gated_grad_t, att_grad_t, w_kv),
        (((5 * width, C), BF16), ((TILE, C), BF16), ((keys, C), BF16)),
        [
            pltpu.VMEM((keys, C), BF16), pltpu.VMEM((keys, 2 * wide), F32),
            pltpu.VMEM((keys, wide), BF16), pltpu.VMEM((keys, 2 * wide), BF16),
        ],
    )

    def summed(one, two):
        return (one.astype(F32) + two.astype(F32)).astype(BF16)

    keep, send = on_core(
        parts_kernel, "parts", [SMEM, SMEM], (col, head, key_value_grad, local, w_qg, w_kv),
        (((wide, C), F32), ((wide, C), BF16)), [pltpu.VMEM((keys, C), F32)],
    )
    half = TILE // 2
    raw = summed(raw, exchange(raw, staggered(other_row, next_col)))
    given = exchange(send, other_head)
    keep, send = on_core(
        fold_kernel, "fold_heads", [], (keep, given), (((TILE, C), F32), ((TILE, C), BF16)),
    )
    raw, keep = lax.optimization_barrier((raw, keep))
    given = exchange(send, next_col)
    send = (keep[half:] + given[half:].astype(F32)).astype(BF16)
    keep, early = keep[:half], given[:half]
    raw = summed(raw, exchange(raw, staggered(far_col, other_row)))
    raw, keep = lax.optimization_barrier((raw, keep))
    given = exchange(send, far_col)
    keep = keep + early.astype(F32)
    last = exchange(raw, staggered(next_col, far_col))
    total, squares = on_core(
        squares_kernel, "squares", [], (raw, last), (((5 * width, C), F32), ((8, C), F32)),
    )
    grads = on_core(
        clip_kernel, "clip", [], (total, squares, exchange(squares, other_head), keep, given),
        (((width, C), F32),) * 5 + (((half, C), BF16),),
    )
    query_grad, gate_grad, key_grad, value_grad, out_weight_grad, pair_grad = grads
    return (
        pair_grad.reshape(1, half, C),
        query_grad.T,
        key_grad.T,
        value_grad.T,
        gate_grad.T,
        out_weight_grad,
    )


def per_device(pair, out_grad, pair_bias, *rest):
    small = lax.axis_size("col") == 4 and lax.axis_size("row") == 2 and lax.axis_size("head") == 2
    if small and pair.shape == (1, TILE, C) and pair_bias.shape == (TILE, 2, 4 * TILE):
        return four_cols(pair, out_grad, pair_bias, *rest)
    return any_cols(pair, out_grad, pair_bias, *rest)


def solution(mesh):
    return jax.shard_map(
        per_device,
        mesh=mesh,
        in_specs=(
            P(("groups", "row"), "col", None),
            P(("groups", "row"), "col", None),
            P(("groups", "col"), "head", None),
            P(None, "head"),
            P(None, "head"),
            P(None, "head"),
            P(None, "head"),
            P("head", None),
            P("groups", None),
            P("groups"),
        ),
        out_specs=(
            P(("groups", "row"), ("col", "head"), None),
            P("groups", "head"),
            P("groups", "head"),
            P("groups", "head"),
            P("groups", "head"),
            P(("groups", "head"), None),
        ),
        check_vma=False,
    )
```

```python
import math

import jax
import jax.numpy as jnp
from jax import lax
from jax.experimental import pallas as pl
from jax.experimental.pallas import tpu as pltpu
from jax.sharding import PartitionSpec as P

C = 128
H = 4
HD = 32
TILE = 128


NEG_FILL = -1e30
F32 = jnp.float32
BF16 = jnp.bfloat16
CLIP_NORM = 0.5 * math.sqrt(5.0 * C * H * HD)


def shifted(value, axis, steps):
    count = lax.axis_size(axis)
    pairs = [(source, (source + steps) % count) for source in range(count)]
    return lax.ppermute(value, axis, pairs)


def allowed_between(tile_mask, chain_ids, query_start, query_count, key_start, key_count):
    tile_ids = jnp.arange(tile_mask.shape[0], dtype=jnp.int32)
    query_pos = query_start + jnp.arange(query_count, dtype=jnp.int32)
    key_pos = key_start + jnp.arange(key_count, dtype=jnp.int32)
    query_tiles = (query_pos[:, None] // TILE == tile_ids[None, :]).astype(jnp.float32)
    key_tiles = (key_pos[:, None] // TILE == tile_ids[None, :]).astype(jnp.float32)
    marks = jnp.dot(jnp.dot(query_tiles, tile_mask.astype(jnp.float32)), key_tiles.T)
    query_chain = lax.dynamic_slice_in_dim(chain_ids, query_start, query_count)
    key_chain = lax.dynamic_slice_in_dim(chain_ids, key_start, key_count)
    return (marks > 0.5) | (query_chain[:, None] == key_chain[None, :])


def score_block(query_four, key_four, bias_block, allowed):
    scores = jnp.einsum("rjhd,rkhd->rjhk", query_four, key_four, preferred_element_type=jnp.float32)
    scores = scores + bias_block[None].astype(jnp.float32)
    return jnp.where(allowed[None, :, None, :], scores, NEG_FILL)


def prob_and_grad(
    query_four, grad_four, log_total, delta_sum, key_four, value_four, bias_block, allowed
):
    scores = score_block(query_four, key_four, bias_block, allowed)
    prob = jnp.where(allowed[None, :, None, :], jnp.exp(scores - log_total[..., None]), 0.0)
    grad_prob = jnp.einsum(
        "rjhd,rkhd->rjhk", grad_four, value_four, preferred_element_type=jnp.float32
    )
    grad_score = (prob * (grad_prob - delta_sum[..., None])).astype(jnp.bfloat16)
    return (prob.astype(jnp.bfloat16), grad_score)


def any_cols(
    pair, out_grad, pair_bias, w_query, w_key, w_value, w_gate, w_out, tile_mask, chain_ids
):
    rows_dev, cols_dev, channels = pair.shape
    heads_dev = pair_bias.shape[1]
    head_width = w_query.shape[1]
    head_size = head_width // heads_dev
    hd_scale = head_size ** (-0.5)
    col_count = lax.axis_size("col")
    col_index = lax.axis_index("col")
    col_start = col_index * cols_dev
    shape_four = (rows_dev, cols_dev, heads_dev, head_size)
    stat_shape = (rows_dev, cols_dev, heads_dev)
    flat_pair = pair.reshape(rows_dev * cols_dev, channels)
    flat_grad = out_grad.reshape(rows_dev * cols_dev, channels)
    w_joined = jnp.concatenate([w_query, w_key, w_value, w_gate], axis=1)
    projected = jnp.dot(flat_pair, w_joined, preferred_element_type=jnp.float32)
    query_flat = (projected[:, :head_width] * hd_scale).astype(jnp.bfloat16)
    key_grid = (
        projected[:, head_width : 2 * head_width]
        .astype(jnp.bfloat16)
        .reshape(rows_dev, cols_dev, head_width)
    )
    value_grid = (
        projected[:, 2 * head_width : 3 * head_width]
        .astype(jnp.bfloat16)
        .reshape(rows_dev, cols_dev, head_width)
    )
    gate_value = jax.nn.sigmoid(projected[:, 3 * head_width :])
    query_four = query_flat.reshape(shape_four)
    key_piece = lax.all_gather(key_grid, "col", axis=1, tiled=True)
    value_piece = lax.all_gather(value_grid, "col", axis=1, tiled=True)
    key_count = key_piece.shape[1]
    allowed = allowed_between(tile_mask, chain_ids, col_start, cols_dev, jnp.int32(0), key_count)
    bias_block = pair_bias
    run_max = jnp.full(stat_shape, NEG_FILL, jnp.float32)
    key_four = key_piece.reshape(rows_dev, key_count, heads_dev, head_size)
    value_four = value_piece.reshape(rows_dev, key_count, heads_dev, head_size)
    scores = score_block(query_four, key_four, bias_block, allowed)
    new_max = jnp.maximum(run_max, jnp.max(scores, axis=3))
    weights = jnp.where(allowed[None, :, None, :], jnp.exp(scores - new_max[..., None]), 0.0)
    new_sum = jnp.sum(weights, axis=3)
    added = jnp.einsum(
        "rjhk,rkhd->rjhd",
        weights.astype(jnp.bfloat16),
        value_four,
        preferred_element_type=jnp.float32,
    )
    attended = (added / new_sum[..., None]).reshape(rows_dev * cols_dev, head_width)
    log_total = new_max + jnp.log(new_sum)
    gated = (gate_value * attended).astype(jnp.bfloat16)
    grad_gated = jnp.dot(flat_grad, w_out.T, preferred_element_type=jnp.float32)
    grad_att = (grad_gated * gate_value).astype(jnp.bfloat16)
    grad_gate_logit = (grad_gated * attended * gate_value * (1.0 - gate_value)).astype(jnp.bfloat16)
    delta_sum = jnp.sum((grad_att.astype(jnp.float32) * attended).reshape(shape_four), axis=3)
    grad_four = grad_att.reshape(shape_four)

    def back_turn(turn_index, loop_state):
        travel_keys, travel_grads, query_acc = loop_state
        owner_col = jnp.mod(col_index - turn_index, col_count)
        key_start = owner_col * cols_dev
        allowed = allowed_between(tile_mask, chain_ids, col_start, cols_dev, key_start, cols_dev)
        bias_block = lax.dynamic_slice_in_dim(pair_bias, key_start, cols_dev, 2)
        grads_in = travel_grads
        query_in = query_acc
        key_four = travel_keys[0].reshape(shape_four)
        value_four = travel_keys[1].reshape(shape_four)
        prob_bf, grad_score = prob_and_grad(
            query_four, grad_four, log_total, delta_sum, key_four, value_four, bias_block, allowed
        )
        query_more = jnp.einsum(
            "rjhk,rkhd->rjhd", grad_score, key_four, preferred_element_type=jnp.float32
        )
        key_more = jnp.einsum(
            "rjhk,rjhd->rkhd", grad_score, query_four, preferred_element_type=jnp.float32
        )
        value_more = jnp.einsum(
            "rjhk,rjhd->rkhd", prob_bf, grad_four, preferred_element_type=jnp.float32
        )
        travel_grads = grads_in + jnp.stack([key_more, value_more]).reshape(grads_in.shape)
        query_acc = query_in + query_more
        travel_keys = shifted(travel_keys, "col", 1)
        travel_grads = shifted(travel_grads.astype(jnp.bfloat16), "col", 1).astype(
            travel_grads.dtype
        )
        return (travel_keys, travel_grads, query_acc)

    def back_pair(pair_index, loop_state):
        for half_turn in range(2):
            loop_state = back_turn(2 * pair_index + half_turn, loop_state)
        return loop_state

    loop_start = (
        jnp.stack([key_grid, value_grid]),
        jnp.zeros((2, rows_dev, cols_dev, head_width), jnp.float32),
        jnp.zeros(shape_four, jnp.float32),
    )
    travel_keys, key_value_acc, query_acc = lax.fori_loop(0, col_count // 2, back_pair, loop_start)
    query_grad = (
        (query_acc * hd_scale).astype(jnp.bfloat16).reshape(rows_dev * cols_dev, head_width)
    )
    key_grad = key_value_acc[0].astype(jnp.bfloat16).reshape(rows_dev * cols_dev, head_width)
    value_grad = key_value_acc[1].astype(jnp.bfloat16).reshape(rows_dev * cols_dev, head_width)
    grad_joined = jnp.concatenate([query_grad, key_grad, value_grad, grad_gate_logit], axis=1)
    partial_pair = jnp.dot(grad_joined, w_joined.T, preferred_element_type=jnp.float32).reshape(
        rows_dev, cols_dev, channels
    )
    pair_grad = lax.psum_scatter(
        partial_pair.astype(jnp.bfloat16), "head", scatter_dimension=1, tiled=True
    )
    raw_four = jnp.dot(flat_pair.T, grad_joined, preferred_element_type=jnp.float32)
    raw_out = jnp.dot(gated.T, flat_grad, preferred_element_type=jnp.float32)
    summed_four, summed_out = lax.psum((raw_four, raw_out), ("col", "row"))
    local_squares = jnp.sum(summed_four * summed_four) + jnp.sum(summed_out * summed_out)
    squares = lax.psum(local_squares, "head")
    clip = jnp.minimum(1.0, 0.5 * math.sqrt(5.0 * C * H * HD) / jnp.sqrt(squares + 1e-06))
    return (
        pair_grad,
        summed_four[:, :head_width] * clip,
        summed_four[:, head_width : 2 * head_width] * clip,
        summed_four[:, 2 * head_width : 3 * head_width] * clip,
        summed_four[:, 3 * head_width :] * clip,
        summed_out * clip,
    )


def exchange(value, partner):
    cols, rows, heads = lax.axis_size("col"), lax.axis_size("row"), lax.axis_size("head")
    pairs = []
    for col in range(cols):
        for row in range(rows):
            for head in range(heads):
                to_col, to_row, to_head = partner(col, row, head)
                source = (col * rows + row) * heads + head
                pairs.append((source, (to_col * rows + to_row) * heads + to_head))
    return lax.ppermute(value, ("col", "row", "head"), pairs)


def next_col(col, row, head):
    return col ^ 1, row, head


def far_col(col, row, head):
    return col ^ 2, row, head


def end_col(col, row, head):
    return col ^ 3, row, head


def other_row(col, row, head):
    return col, row ^ 1, head


def other_head(col, row, head):
    return col, row, head ^ 1


def staggered(first, second):
    return lambda col, row, head: (first, second)[head](col, row, head)


def dot_nn(left, right):
    return jnp.dot(left, right, preferred_element_type=F32)


def dot_nt(left, right):
    return lax.dot_general(left, right, (((1,), (1,)), ((), ())), preferred_element_type=F32)


def split_rows(flat):
    first = lax.broadcasted_iota(jnp.int32, flat.shape, 0) < HD
    zero = jnp.zeros_like(flat)
    return jnp.concatenate([jnp.where(first, flat, zero), jnp.where(first, zero, flat)], axis=1)


def join_rows(wide):
    count = wide.shape[1] // 2
    first = lax.broadcasted_iota(jnp.int32, (wide.shape[0], count), 0) < HD
    return jnp.where(first, wide[:, :count], wide[:, count:])


def split_cols(flat):
    first = lax.broadcasted_iota(jnp.int32, flat.shape, 1) < HD
    zero = jnp.zeros_like(flat)
    return jnp.concatenate([jnp.where(first, flat, zero), jnp.where(first, zero, flat)], axis=0)


def local_kernel(
    col_ref, tile_hbm, x_hbm, grad_hbm, bias_hbm, chain_hbm, wq_hbm, wk_hbm, wv_hbm, wg_hbm, wo_hbm,
    x_ref, grad_ref, w_qg_ref, w_kv_ref, bias_out, left_out, right_out, gate_out, gated_grad_out,
    att_grad_out, tile_ref, chain_ref, wo_ref, bias_ref, sems,
):
    scale = HD ** (-0.5)
    width = 2 * TILE
    me = col_ref[0]
    moves = [
        (x_hbm, x_ref),
        (wq_hbm, w_qg_ref.at[: 2 * HD]),
        (wg_hbm, w_qg_ref.at[2 * HD :]),
        (grad_hbm, grad_ref),
        (wo_hbm, wo_ref),
        (chain_hbm, chain_ref),
        (tile_hbm, tile_ref),
        (bias_hbm, bias_ref),
        (wk_hbm, w_kv_ref.at[: 2 * HD]),
        (wv_hbm, w_kv_ref.at[2 * HD :]),
    ]
    copies = [
        pltpu.make_async_copy(source, target, sems.at[place])
        for place, (source, target) in enumerate(moves)
    ]
    for copy in copies:
        copy.start()
    for copy in copies[:5]:
        copy.wait()
    x = x_ref[...]
    query_gate = dot_nt(w_qg_ref[...], x)
    gated_grad_t = dot_nt(wo_ref[...], grad_ref[...])
    query = (dot_nt(x, w_qg_ref[: 2 * HD, :]) * scale).astype(BF16)
    query_t = (query_gate[: 2 * HD] * scale).astype(BF16)
    gate_t = jax.nn.sigmoid(query_gate[2 * HD :])
    att_grad_t = (gated_grad_t * gate_t).astype(BF16)
    att_grad_f = att_grad_t.astype(F32)
    att_grad = jnp.transpose(att_grad_f).astype(BF16)
    zero_wide = jnp.zeros((2 * HD, width), BF16)
    zero_tall = jnp.zeros((width, 2 * HD), BF16)
    left_out[: 2 * HD, :] = jnp.concatenate([split_rows(query_t), zero_wide], axis=1)
    left_out[2 * HD :, :] = jnp.concatenate([zero_wide, split_rows(att_grad_t)], axis=1)
    right_out[:width, :] = jnp.concatenate([split_cols(query), zero_tall], axis=1)
    right_out[width:, :] = jnp.concatenate([zero_tall, split_cols(att_grad)], axis=1)
    gate_out[...] = gate_t
    gated_grad_out[...] = gated_grad_t
    att_grad_out[...] = att_grad_f
    for copy in copies[5:]:
        copy.wait()
    chains = chain_ref[...].astype(F32)
    own_chain = chain_ref[pl.ds(me, 1), :].astype(F32)
    for block in range(4):
        rows = slice(block * TILE, (block + 1) * TILE)
        key_chain = jnp.transpose(jnp.broadcast_to(chains[block : block + 1, :], (TILE, TILE)))
        apart = jnp.where(tile_ref[me, block] == 1, 0.0, 1.0)
        banned = jnp.where(key_chain == own_chain, 0.0, apart) > 0.5
        for head in range(2):
            bias = bias_ref[:, head, rows].astype(F32)
            bias_out[rows, head * TILE : (head + 1) * TILE] = jnp.where(
                banned, NEG_FILL, jnp.transpose(bias)
            )


def attention_kernel(
    col_ref, head_ref, x_ref, next_ref, direct_ref, crossed_ref, grad_ref, bias_ref, left_ref, right_ref,
    gate_ref, gated_grad_ref, att_grad_ref, w_kv_ref,
    raw_ref, local_ref, key_value_grad_ref,
    pairs_ref, scores_ref, expo_ref, both_ref,
):
    scale = HD ** (-0.5)
    width = 2 * TILE
    me, head = col_ref[0], head_ref[0]
    for bits, ref in ((0, x_ref), (1, next_ref), (2 + head, direct_ref), (3 - head, crossed_ref)):
        place = pl.multiple_of(lax.bitwise_xor(me, bits) * TILE, TILE)
        pairs_ref[pl.ds(place, TILE), :] = ref[...]
    w_kv = w_kv_ref[...]
    pairs = pairs_ref[...]
    key_value = dot_nt(pairs, w_kv).astype(BF16)
    key_value_t = dot_nt(w_kv, pairs).astype(BF16)
    left = left_ref[...]
    top = None
    for block in range(4):
        rows = slice(block * TILE, (block + 1) * TILE)
        product = dot_nn(key_value[rows], left)
        scores = product[:, :width] + bias_ref[rows, :]
        scores_ref[rows, :width] = scores
        scores_ref[rows, width:] = product[:, width:]
        part = jnp.max(scores.reshape(TILE // 8, 8, width), axis=0)
        top = part if top is None else jnp.maximum(top, part)
    top = jnp.max(top, axis=0, keepdims=True)
    total = jnp.zeros((8, width), F32)
    for block in range(4):
        rows = slice(block * TILE, (block + 1) * TILE)
        expo = jnp.exp(scores_ref[rows, :width] - top)
        scores_ref[rows, :width] = expo
        expo_ref[rows, :] = expo.astype(BF16)
        total = total + jnp.sum(expo.reshape(TILE // 8, 8, width), axis=0)
    inverse = 1.0 / jnp.sum(total, axis=0, keepdims=True)
    attended_t = join_rows(dot_nn(key_value_t[2 * HD :], expo_ref[...]) * inverse)
    gate_t, gated_grad_t = gate_ref[...], gated_grad_ref[...]
    gated_t = (gate_t * attended_t).astype(BF16)
    gate_logit_t = gated_grad_t * attended_t * gate_t * (1.0 - gate_t)
    products = att_grad_ref[...] * attended_t
    delta = jnp.concatenate(
        [
            jnp.sum(products[:HD], axis=0, keepdims=True),
            jnp.sum(products[HD:], axis=0, keepdims=True),
        ],
        axis=1,
    )
    for block in range(4):
        rows = slice(block * TILE, (block + 1) * TILE)
        prob = scores_ref[rows, :width] * inverse
        both_ref[rows, :width] = (prob * (scores_ref[rows, width:] - delta)).astype(BF16)
        both_ref[rows, width:] = prob.astype(BF16)
    query_grad_t = join_rows(dot_nn(key_value_t[: 2 * HD], both_ref[:, :width])) * scale
    key_value_grad = dot_nn(both_ref[...], right_ref[...])
    local_t = jnp.concatenate([query_grad_t, gate_logit_t], axis=0)
    local_ref[...] = jnp.transpose(local_t).astype(BF16)
    key_value_grad_ref[...] = key_value_grad.astype(BF16)
    raw_ref[: 4 * HD, :] = dot_nn(local_t.astype(BF16), x_ref[...]).astype(BF16)
    raw_ref[4 * HD : 8 * HD, :] = dot_nn(jnp.transpose(key_value_grad).astype(BF16), pairs).astype(BF16)
    raw_ref[8 * HD :, :] = dot_nn(gated_t, grad_ref[...]).astype(BF16)


def parts_kernel(
    col_ref, head_ref, key_value_grad_ref, local_ref, w_qg_ref, w_kv_ref, keep_ref, send_ref, parts_ref
):
    me, head = col_ref[0], head_ref[0]
    half = TILE // 2
    parts_ref[...] = dot_nn(key_value_grad_ref[...], w_kv_ref[...])
    own = pl.ds(pl.multiple_of(me * TILE, TILE), TILE)
    parts_ref[own, :] = parts_ref[own, :] + dot_nn(local_ref[...], w_qg_ref[...])
    for place, bits in enumerate((0, 2, 1, 3)):
        start = lax.bitwise_xor(me, bits) * TILE
        mine = pl.multiple_of(start + head * half, half)
        other = pl.multiple_of(start + (1 - head) * half, half)
        rows = slice(place * half, (place + 1) * half)
        keep_ref[rows, :] = parts_ref[pl.ds(mine, half), :]
        send_ref[rows, :] = parts_ref[pl.ds(other, half), :].astype(BF16)


def fold_kernel(own_ref, other_ref, keep_ref, send_ref):
    half = keep_ref.shape[0]
    keep_ref[...] = own_ref[:half, :] + other_ref[:half, :].astype(F32)
    send_ref[...] = (own_ref[half:, :] + other_ref[half:, :].astype(F32)).astype(BF16)


def squares_kernel(own_ref, other_ref, total_ref, squares_ref):
    total = own_ref[...].astype(F32) + other_ref[...].astype(F32)
    total_ref[...] = total
    squares_ref[...] = jnp.sum((total * total).reshape(total.shape[0] // 8, 8, C), axis=0)


def clip_kernel(
    total_ref, own_ref, other_ref, pair_own_ref, pair_other_ref,
    query_ref, gate_ref, key_ref, value_ref, out_ref, pair_ref,
):
    squares = own_ref[...] + other_ref[...]
    squares = jnp.sum(jnp.sum(squares, axis=0, keepdims=True), axis=1, keepdims=True)
    clip = jnp.minimum(1.0, CLIP_NORM / jnp.sqrt(squares + 1e-06))
    for part, ref in enumerate((query_ref, gate_ref, key_ref, value_ref, out_ref)):
        ref[...] = total_ref[part * 2 * HD : (part + 1) * 2 * HD, :] * clip
    pair_ref[...] = (pair_own_ref[...] + pair_other_ref[...].astype(F32)).astype(BF16)


VMEM = pl.BlockSpec(memory_space=pltpu.VMEM)
SMEM = pl.BlockSpec(memory_space=pltpu.SMEM)
HBM = pl.BlockSpec(memory_space=pltpu.HBM)


def on_core(kernel, name, specs, operands, outs, scratch=(), cost=1 << 18):
    return pl.pallas_call(
        kernel,
        out_shape=tuple(jax.ShapeDtypeStruct(shape, dtype) for shape, dtype in outs),
        in_specs=specs + [VMEM] * (len(operands) - len(specs)),
        out_specs=(VMEM,) * len(outs),
        scratch_shapes=scratch,
        compiler_params=pltpu.CompilerParams(vmem_limit_bytes=16 << 20),
        cost_estimate=pl.CostEstimate(flops=1 << 20, bytes_accessed=cost, transcendentals=0),
        name=name,
    )(
        *(
            pltpu.with_memory_space_constraint(operand, pltpu.HBM) if spec is HBM else operand
            for spec, operand in zip(specs + [VMEM] * len(operands), operands)
        )
    )


def four_cols(
    pair, out_grad, pair_bias, w_query, w_key, w_value, w_gate, w_out, tile_mask, chain_ids
):
    col_index = lax.axis_index("col")
    head_index = lax.axis_index("head")
    col = col_index.reshape(1)
    width, keys, wide = 2 * HD, 4 * TILE, 2 * TILE
    x = pair.reshape(TILE, C)
    head = head_index.reshape(1)
    x_direct = exchange(x, staggered(far_col, end_col))
    x_next = exchange(x, next_col)
    x, grad, w_qg, w_kv, bias, left, right, gate_t, gated_grad_t, att_grad_t = on_core(
        local_kernel, "local", [SMEM] + [HBM] * 10,
        (
            col, tile_mask, x, out_grad.reshape(TILE, C), pair_bias, chain_ids.reshape(4, TILE),
            w_query.T, w_key.T, w_value.T, w_gate.T, w_out,
        ),
        (
            ((TILE, C), BF16), ((TILE, C), BF16), ((2 * width, C), BF16), ((2 * width, C), BF16),
            ((keys, wide), F32), ((C, 2 * wide), BF16), ((2 * wide, C), BF16),
            ((width, TILE), F32), ((width, TILE), F32), ((width, TILE), F32),
        ),
        [
            pltpu.SMEM((4, 4), jnp.int32), pltpu.VMEM((4, TILE), jnp.int32),
            pltpu.VMEM((width, C), BF16), pltpu.VMEM((TILE, 2, keys), BF16),
            pltpu.SemaphoreType.DMA((10,)),
        ],
    )
    x_direct, w_kv = lax.optimization_barrier((x_direct, w_kv))
    x_crossed = exchange(x_direct, other_head)
    raw, local, key_value_grad = on_core(
        attention_kernel, "attention", [SMEM, SMEM],
        (col, head, x, x_next, x_direct, x_crossed, grad, bias, left, right, gate_t, gated_grad_t, att_grad_t, w_kv),
        (((5 * width, C), BF16), ((TILE, C), BF16), ((keys, C), BF16)),
        [
            pltpu.VMEM((keys, C), BF16), pltpu.VMEM((keys, 2 * wide), F32),
            pltpu.VMEM((keys, wide), BF16), pltpu.VMEM((keys, 2 * wide), BF16),
        ],
    )

    def summed(one, two):
        return (one.astype(F32) + two.astype(F32)).astype(BF16)

    keep, send = on_core(
        parts_kernel, "parts", [SMEM, SMEM], (col, head, key_value_grad, local, w_qg, w_kv),
        (((wide, C), F32), ((wide, C), BF16)), [pltpu.VMEM((keys, C), F32)],
    )
    half = TILE // 2
    raw = summed(raw, exchange(raw, staggered(next_col, far_col)))
    given = exchange(send, other_head)
    keep, send = on_core(
        fold_kernel, "fold_heads", [], (keep, given), (((TILE, C), F32), ((TILE, C), BF16)),
    )
    raw, keep = lax.optimization_barrier((raw, keep))
    given = exchange(send, next_col)
    send = (keep[half:] + given[half:].astype(F32)).astype(BF16)
    keep, early = keep[:half], given[:half]
    raw = summed(raw, exchange(raw, staggered(far_col, other_row)))
    raw, keep = lax.optimization_barrier((raw, keep))
    given = exchange(send, far_col)
    keep = keep + early.astype(F32)
    last = exchange(raw, staggered(other_row, next_col))
    total, squares = on_core(
        squares_kernel, "squares", [], (raw, last), (((5 * width, C), F32), ((8, C), F32)),
    )
    grads = on_core(
        clip_kernel, "clip", [], (total, squares, exchange(squares, other_head), keep, given),
        (((width, C), F32),) * 5 + (((half, C), BF16),),
    )
    query_grad, gate_grad, key_grad, value_grad, out_weight_grad, pair_grad = grads
    return (
        pair_grad.reshape(1, half, C),
        query_grad.T,
        key_grad.T,
        value_grad.T,
        gate_grad.T,
        out_weight_grad,
    )


def per_device(pair, out_grad, pair_bias, *rest):
    small = lax.axis_size("col") == 4 and lax.axis_size("row") == 2 and lax.axis_size("head") == 2
    if small and pair.shape == (1, TILE, C) and pair_bias.shape == (TILE, 2, 4 * TILE):
        return four_cols(pair, out_grad, pair_bias, *rest)
    return any_cols(pair, out_grad, pair_bias, *rest)


def solution(mesh):
    return jax.shard_map(
        per_device,
        mesh=mesh,
        in_specs=(
            P(("groups", "row"), "col", None),
            P(("groups", "row"), "col", None),
            P(("groups", "col"), "head", None),
            P(None, "head"),
            P(None, "head"),
            P(None, "head"),
            P(None, "head"),
            P("head", None),
            P("groups", None),
            P("groups"),
        ),
        out_specs=(
            P(("groups", "row"), ("col", "head"), None),
            P("groups", "head"),
            P("groups", "head"),
            P("groups", "head"),
            P("groups", "head"),
            P(("groups", "head"), None),
        ),
        check_vma=False,
    )
```

```python
import math

import jax
import jax.numpy as jnp
from jax import lax
from jax.experimental import pallas as pl
from jax.experimental.pallas import tpu as pltpu
from jax.sharding import PartitionSpec as P

C = 128
H = 4
HD = 32
TILE = 128


NEG_FILL = -1e30
F32 = jnp.float32
BF16 = jnp.bfloat16
CLIP_NORM = 0.5 * math.sqrt(5.0 * C * H * HD)


def shifted(value, axis, steps):
    count = lax.axis_size(axis)
    pairs = [(source, (source + steps) % count) for source in range(count)]
    return lax.ppermute(value, axis, pairs)


def allowed_between(tile_mask, chain_ids, query_start, query_count, key_start, key_count):
    tile_ids = jnp.arange(tile_mask.shape[0], dtype=jnp.int32)
    query_pos = query_start + jnp.arange(query_count, dtype=jnp.int32)
    key_pos = key_start + jnp.arange(key_count, dtype=jnp.int32)
    query_tiles = (query_pos[:, None] // TILE == tile_ids[None, :]).astype(jnp.float32)
    key_tiles = (key_pos[:, None] // TILE == tile_ids[None, :]).astype(jnp.float32)
    marks = jnp.dot(jnp.dot(query_tiles, tile_mask.astype(jnp.float32)), key_tiles.T)
    query_chain = lax.dynamic_slice_in_dim(chain_ids, query_start, query_count)
    key_chain = lax.dynamic_slice_in_dim(chain_ids, key_start, key_count)
    return (marks > 0.5) | (query_chain[:, None] == key_chain[None, :])


def score_block(query_four, key_four, bias_block, allowed):
    scores = jnp.einsum("rjhd,rkhd->rjhk", query_four, key_four, preferred_element_type=jnp.float32)
    scores = scores + bias_block[None].astype(jnp.float32)
    return jnp.where(allowed[None, :, None, :], scores, NEG_FILL)


def prob_and_grad(
    query_four, grad_four, log_total, delta_sum, key_four, value_four, bias_block, allowed
):
    scores = score_block(query_four, key_four, bias_block, allowed)
    prob = jnp.where(allowed[None, :, None, :], jnp.exp(scores - log_total[..., None]), 0.0)
    grad_prob = jnp.einsum(
        "rjhd,rkhd->rjhk", grad_four, value_four, preferred_element_type=jnp.float32
    )
    grad_score = (prob * (grad_prob - delta_sum[..., None])).astype(jnp.bfloat16)
    return (prob.astype(jnp.bfloat16), grad_score)


def any_cols(
    pair, out_grad, pair_bias, w_query, w_key, w_value, w_gate, w_out, tile_mask, chain_ids
):
    rows_dev, cols_dev, channels = pair.shape
    heads_dev = pair_bias.shape[1]
    head_width = w_query.shape[1]
    head_size = head_width // heads_dev
    hd_scale = head_size ** (-0.5)
    col_count = lax.axis_size("col")
    col_index = lax.axis_index("col")
    col_start = col_index * cols_dev
    shape_four = (rows_dev, cols_dev, heads_dev, head_size)
    stat_shape = (rows_dev, cols_dev, heads_dev)
    flat_pair = pair.reshape(rows_dev * cols_dev, channels)
    flat_grad = out_grad.reshape(rows_dev * cols_dev, channels)
    w_joined = jnp.concatenate([w_query, w_key, w_value, w_gate], axis=1)
    projected = jnp.dot(flat_pair, w_joined, preferred_element_type=jnp.float32)
    query_flat = (projected[:, :head_width] * hd_scale).astype(jnp.bfloat16)
    key_grid = (
        projected[:, head_width : 2 * head_width]
        .astype(jnp.bfloat16)
        .reshape(rows_dev, cols_dev, head_width)
    )
    value_grid = (
        projected[:, 2 * head_width : 3 * head_width]
        .astype(jnp.bfloat16)
        .reshape(rows_dev, cols_dev, head_width)
    )
    gate_value = jax.nn.sigmoid(projected[:, 3 * head_width :])
    query_four = query_flat.reshape(shape_four)
    key_piece = lax.all_gather(key_grid, "col", axis=1, tiled=True)
    value_piece = lax.all_gather(value_grid, "col", axis=1, tiled=True)
    key_count = key_piece.shape[1]
    allowed = allowed_between(tile_mask, chain_ids, col_start, cols_dev, jnp.int32(0), key_count)
    bias_block = pair_bias
    run_max = jnp.full(stat_shape, NEG_FILL, jnp.float32)
    key_four = key_piece.reshape(rows_dev, key_count, heads_dev, head_size)
    value_four = value_piece.reshape(rows_dev, key_count, heads_dev, head_size)
    scores = score_block(query_four, key_four, bias_block, allowed)
    new_max = jnp.maximum(run_max, jnp.max(scores, axis=3))
    weights = jnp.where(allowed[None, :, None, :], jnp.exp(scores - new_max[..., None]), 0.0)
    new_sum = jnp.sum(weights, axis=3)
    added = jnp.einsum(
        "rjhk,rkhd->rjhd",
        weights.astype(jnp.bfloat16),
        value_four,
        preferred_element_type=jnp.float32,
    )
    attended = (added / new_sum[..., None]).reshape(rows_dev * cols_dev, head_width)
    log_total = new_max + jnp.log(new_sum)
    gated = (gate_value * attended).astype(jnp.bfloat16)
    grad_gated = jnp.dot(flat_grad, w_out.T, preferred_element_type=jnp.float32)
    grad_att = (grad_gated * gate_value).astype(jnp.bfloat16)
    grad_gate_logit = (grad_gated * attended * gate_value * (1.0 - gate_value)).astype(jnp.bfloat16)
    delta_sum = jnp.sum((grad_att.astype(jnp.float32) * attended).reshape(shape_four), axis=3)
    grad_four = grad_att.reshape(shape_four)

    def back_turn(turn_index, loop_state):
        travel_keys, travel_grads, query_acc = loop_state
        owner_col = jnp.mod(col_index - turn_index, col_count)
        key_start = owner_col * cols_dev
        allowed = allowed_between(tile_mask, chain_ids, col_start, cols_dev, key_start, cols_dev)
        bias_block = lax.dynamic_slice_in_dim(pair_bias, key_start, cols_dev, 2)
        grads_in = travel_grads
        query_in = query_acc
        key_four = travel_keys[0].reshape(shape_four)
        value_four = travel_keys[1].reshape(shape_four)
        prob_bf, grad_score = prob_and_grad(
            query_four, grad_four, log_total, delta_sum, key_four, value_four, bias_block, allowed
        )
        query_more = jnp.einsum(
            "rjhk,rkhd->rjhd", grad_score, key_four, preferred_element_type=jnp.float32
        )
        key_more = jnp.einsum(
            "rjhk,rjhd->rkhd", grad_score, query_four, preferred_element_type=jnp.float32
        )
        value_more = jnp.einsum(
            "rjhk,rjhd->rkhd", prob_bf, grad_four, preferred_element_type=jnp.float32
        )
        travel_grads = grads_in + jnp.stack([key_more, value_more]).reshape(grads_in.shape)
        query_acc = query_in + query_more
        travel_keys = shifted(travel_keys, "col", 1)
        travel_grads = shifted(travel_grads.astype(jnp.bfloat16), "col", 1).astype(
            travel_grads.dtype
        )
        return (travel_keys, travel_grads, query_acc)

    def back_pair(pair_index, loop_state):
        for half_turn in range(2):
            loop_state = back_turn(2 * pair_index + half_turn, loop_state)
        return loop_state

    loop_start = (
        jnp.stack([key_grid, value_grid]),
        jnp.zeros((2, rows_dev, cols_dev, head_width), jnp.float32),
        jnp.zeros(shape_four, jnp.float32),
    )
    travel_keys, key_value_acc, query_acc = lax.fori_loop(0, col_count // 2, back_pair, loop_start)
    query_grad = (
        (query_acc * hd_scale).astype(jnp.bfloat16).reshape(rows_dev * cols_dev, head_width)
    )
    key_grad = key_value_acc[0].astype(jnp.bfloat16).reshape(rows_dev * cols_dev, head_width)
    value_grad = key_value_acc[1].astype(jnp.bfloat16).reshape(rows_dev * cols_dev, head_width)
    grad_joined = jnp.concatenate([query_grad, key_grad, value_grad, grad_gate_logit], axis=1)
    partial_pair = jnp.dot(grad_joined, w_joined.T, preferred_element_type=jnp.float32).reshape(
        rows_dev, cols_dev, channels
    )
    pair_grad = lax.psum_scatter(
        partial_pair.astype(jnp.bfloat16), "head", scatter_dimension=1, tiled=True
    )
    raw_four = jnp.dot(flat_pair.T, grad_joined, preferred_element_type=jnp.float32)
    raw_out = jnp.dot(gated.T, flat_grad, preferred_element_type=jnp.float32)
    summed_four, summed_out = lax.psum((raw_four, raw_out), ("col", "row"))
    local_squares = jnp.sum(summed_four * summed_four) + jnp.sum(summed_out * summed_out)
    squares = lax.psum(local_squares, "head")
    clip = jnp.minimum(1.0, 0.5 * math.sqrt(5.0 * C * H * HD) / jnp.sqrt(squares + 1e-06))
    return (
        pair_grad,
        summed_four[:, :head_width] * clip,
        summed_four[:, head_width : 2 * head_width] * clip,
        summed_four[:, 2 * head_width : 3 * head_width] * clip,
        summed_four[:, 3 * head_width :] * clip,
        summed_out * clip,
    )


def exchange(value, partner):
    cols, rows, heads = lax.axis_size("col"), lax.axis_size("row"), lax.axis_size("head")
    pairs = []
    for col in range(cols):
        for row in range(rows):
            for head in range(heads):
                to_col, to_row, to_head = partner(col, row, head)
                source = (col * rows + row) * heads + head
                pairs.append((source, (to_col * rows + to_row) * heads + to_head))
    return lax.ppermute(value, ("col", "row", "head"), pairs)


def next_col(col, row, head):
    return col ^ 1, row, head


def far_col(col, row, head):
    return col ^ 2, row, head


def end_col(col, row, head):
    return col ^ 3, row, head


def other_row(col, row, head):
    return col, row ^ 1, head


def other_head(col, row, head):
    return col, row, head ^ 1


def staggered(first, second):
    return lambda col, row, head: (first, second)[head](col, row, head)


def dot_nn(left, right):
    return jnp.dot(left, right, preferred_element_type=F32)


def dot_nt(left, right):
    return lax.dot_general(left, right, (((1,), (1,)), ((), ())), preferred_element_type=F32)


def split_rows(flat):
    first = lax.broadcasted_iota(jnp.int32, flat.shape, 0) < HD
    zero = jnp.zeros_like(flat)
    return jnp.concatenate([jnp.where(first, flat, zero), jnp.where(first, zero, flat)], axis=1)


def join_rows(wide):
    count = wide.shape[1] // 2
    first = lax.broadcasted_iota(jnp.int32, (wide.shape[0], count), 0) < HD
    return jnp.where(first, wide[:, :count], wide[:, count:])


def split_cols(flat):
    first = lax.broadcasted_iota(jnp.int32, flat.shape, 1) < HD
    zero = jnp.zeros_like(flat)
    return jnp.concatenate([jnp.where(first, flat, zero), jnp.where(first, zero, flat)], axis=0)


def local_kernel(
    col_ref, tile_hbm, x_hbm, grad_hbm, bias_hbm, chain_hbm, wq_hbm, wk_hbm, wv_hbm, wg_hbm, wo_hbm,
    x_ref, grad_ref, w_qg_ref, w_kv_ref, bias_out, left_out, right_out, gate_out, gated_grad_out,
    tile_ref, chain_ref, wo_ref, bias_ref, sems,
):
    scale = HD ** (-0.5)
    width = 2 * TILE
    me = col_ref[0]
    moves = [
        (x_hbm, x_ref),
        (wq_hbm, w_qg_ref.at[: 2 * HD]),
        (wg_hbm, w_qg_ref.at[2 * HD :]),
        (grad_hbm, grad_ref),
        (wo_hbm, wo_ref),
        (chain_hbm, chain_ref),
        (tile_hbm, tile_ref),
        (bias_hbm, bias_ref),
        (wk_hbm, w_kv_ref.at[: 2 * HD]),
        (wv_hbm, w_kv_ref.at[2 * HD :]),
    ]
    copies = [
        pltpu.make_async_copy(source, target, sems.at[place])
        for place, (source, target) in enumerate(moves)
    ]
    for copy in copies:
        copy.start()
    for copy in copies[:5]:
        copy.wait()
    x = x_ref[...]
    query_gate = dot_nt(w_qg_ref[...], x)
    gated_grad_t = dot_nt(wo_ref[...], grad_ref[...])
    query = (dot_nt(x, w_qg_ref[: 2 * HD, :]) * scale).astype(BF16)
    query_t = (query_gate[: 2 * HD] * scale).astype(BF16)
    gate_t = jax.nn.sigmoid(query_gate[2 * HD :])
    att_grad_t = (gated_grad_t * gate_t).astype(BF16)
    att_grad_f = att_grad_t.astype(F32)
    att_grad = jnp.transpose(att_grad_f).astype(BF16)
    zero_wide = jnp.zeros((2 * HD, width), BF16)
    zero_tall = jnp.zeros((width, 2 * HD), BF16)
    left_out[: 2 * HD, :] = jnp.concatenate([split_rows(query_t), zero_wide], axis=1)
    left_out[2 * HD :, :] = jnp.concatenate([zero_wide, split_rows(att_grad_t)], axis=1)
    right_out[:width, :] = jnp.concatenate([split_cols(query), zero_tall], axis=1)
    right_out[width:, :] = jnp.concatenate([zero_tall, split_cols(att_grad)], axis=1)
    gate_out[...] = gate_t
    gated_grad_out[...] = gated_grad_t
    for copy in copies[5:]:
        copy.wait()
    chains = chain_ref[...].astype(F32)
    own_chain = chain_ref[pl.ds(me, 1), :].astype(F32)
    for block in range(4):
        rows = slice(block * TILE, (block + 1) * TILE)
        key_chain = jnp.transpose(jnp.broadcast_to(chains[block : block + 1, :], (TILE, TILE)))
        apart = jnp.where(tile_ref[me, block] == 1, 0.0, 1.0)
        banned = jnp.where(key_chain == own_chain, 0.0, apart) > 0.5
        for head in range(2):
            bias = bias_ref[:, head, rows].astype(F32)
            bias_out[rows, head * TILE : (head + 1) * TILE] = jnp.where(
                banned, NEG_FILL, jnp.transpose(bias)
            )


def attention_kernel(
    col_ref, head_ref, x_ref, next_ref, direct_ref, crossed_ref, grad_ref, bias_ref, left_ref, right_ref,
    gate_ref, gated_grad_ref, w_kv_ref,
    raw_ref, local_ref, key_value_grad_ref,
    pairs_ref, scores_ref, expo_ref, both_ref,
):
    scale = HD ** (-0.5)
    width = 2 * TILE
    me, head = col_ref[0], head_ref[0]
    for bits, ref in ((0, x_ref), (1, next_ref), (2 + head, direct_ref), (3 - head, crossed_ref)):
        place = pl.multiple_of(lax.bitwise_xor(me, bits) * TILE, TILE)
        pairs_ref[pl.ds(place, TILE), :] = ref[...]
    w_kv = w_kv_ref[...]
    pairs = pairs_ref[...]
    key_value = dot_nt(pairs, w_kv).astype(BF16)
    key_value_t = dot_nt(w_kv, pairs).astype(BF16)
    left = left_ref[...]
    top = None
    for block in range(4):
        rows = slice(block * TILE, (block + 1) * TILE)
        product = dot_nn(key_value[rows], left)
        scores = product[:, :width] + bias_ref[rows, :]
        scores_ref[rows, :width] = scores
        scores_ref[rows, width:] = product[:, width:]
        part = jnp.max(scores.reshape(TILE // 8, 8, width), axis=0)
        top = part if top is None else jnp.maximum(top, part)
    top = jnp.max(top, axis=0, keepdims=True)
    total = jnp.zeros((8, width), F32)
    weighted = jnp.zeros((8, width), F32)
    for block in range(4):
        rows = slice(block * TILE, (block + 1) * TILE)
        expo = jnp.exp(scores_ref[rows, :width] - top)
        scores_ref[rows, :width] = expo
        expo_ref[rows, :] = expo.astype(BF16)
        total = total + jnp.sum(expo.reshape(TILE // 8, 8, width), axis=0)
        products = expo * scores_ref[rows, width:]
        weighted = weighted + jnp.sum(products.reshape(TILE // 8, 8, width), axis=0)
    inverse = 1.0 / jnp.sum(total, axis=0, keepdims=True)
    delta = jnp.sum(weighted, axis=0, keepdims=True) * inverse
    attended_t = join_rows(dot_nn(key_value_t[2 * HD :], expo_ref[...]) * inverse)
    gate_t, gated_grad_t = gate_ref[...], gated_grad_ref[...]
    gated_t = (gate_t * attended_t).astype(BF16)
    gate_logit_t = gated_grad_t * attended_t * gate_t * (1.0 - gate_t)
    for block in range(4):
        rows = slice(block * TILE, (block + 1) * TILE)
        prob = scores_ref[rows, :width] * inverse
        both_ref[rows, :width] = (prob * (scores_ref[rows, width:] - delta)).astype(BF16)
        both_ref[rows, width:] = prob.astype(BF16)
    query_grad_t = join_rows(dot_nn(key_value_t[: 2 * HD], both_ref[:, :width])) * scale
    key_value_grad = dot_nn(both_ref[...], right_ref[...])
    local_t = jnp.concatenate([query_grad_t, gate_logit_t], axis=0)
    local_ref[...] = jnp.transpose(local_t).astype(BF16)
    key_value_grad_ref[...] = key_value_grad.astype(BF16)
    raw_ref[: 4 * HD, :] = dot_nn(local_t.astype(BF16), x_ref[...]).astype(BF16)
    raw_ref[4 * HD : 8 * HD, :] = dot_nn(jnp.transpose(key_value_grad).astype(BF16), pairs).astype(BF16)
    raw_ref[8 * HD :, :] = dot_nn(gated_t, grad_ref[...]).astype(BF16)


def parts_kernel(
    col_ref, head_ref, key_value_grad_ref, local_ref, w_qg_ref, w_kv_ref, keep_ref, send_ref, parts_ref
):
    me, head = col_ref[0], head_ref[0]
    half = TILE // 2
    parts_ref[...] = dot_nn(key_value_grad_ref[...], w_kv_ref[...])
    own = pl.ds(pl.multiple_of(me * TILE, TILE), TILE)
    parts_ref[own, :] = parts_ref[own, :] + dot_nn(local_ref[...], w_qg_ref[...])
    for place, bits in enumerate((0, 2, 1, 3)):
        start = lax.bitwise_xor(me, bits) * TILE
        mine = pl.multiple_of(start + head * half, half)
        other = pl.multiple_of(start + (1 - head) * half, half)
        rows = slice(place * half, (place + 1) * half)
        keep_ref[rows, :] = parts_ref[pl.ds(mine, half), :]
        send_ref[rows, :] = parts_ref[pl.ds(other, half), :].astype(BF16)


def fold_kernel(own_ref, other_ref, keep_ref, send_ref):
    half = keep_ref.shape[0]
    keep_ref[...] = own_ref[:half, :] + other_ref[:half, :].astype(F32)
    send_ref[...] = (own_ref[half:, :] + other_ref[half:, :].astype(F32)).astype(BF16)


def squares_kernel(own_ref, other_ref, total_ref, squares_ref):
    total = own_ref[...].astype(F32) + other_ref[...].astype(F32)
    total_ref[...] = total
    squares_ref[...] = jnp.sum((total * total).reshape(total.shape[0] // 8, 8, C), axis=0)


def clip_kernel(
    total_ref, own_ref, other_ref, pair_own_ref, pair_other_ref,
    query_ref, gate_ref, key_ref, value_ref, out_ref, pair_ref,
):
    squares = own_ref[...] + other_ref[...]
    squares = jnp.sum(jnp.sum(squares, axis=0, keepdims=True), axis=1, keepdims=True)
    clip = jnp.minimum(1.0, CLIP_NORM / jnp.sqrt(squares + 1e-06))
    for part, ref in enumerate((query_ref, gate_ref, key_ref, value_ref, out_ref)):
        ref[...] = total_ref[part * 2 * HD : (part + 1) * 2 * HD, :] * clip
    pair_ref[...] = (pair_own_ref[...] + pair_other_ref[...].astype(F32)).astype(BF16)


VMEM = pl.BlockSpec(memory_space=pltpu.VMEM)
SMEM = pl.BlockSpec(memory_space=pltpu.SMEM)
HBM = pl.BlockSpec(memory_space=pltpu.HBM)


def on_core(kernel, name, specs, operands, outs, scratch=(), cost=1 << 18):
    return pl.pallas_call(
        kernel,
        out_shape=tuple(jax.ShapeDtypeStruct(shape, dtype) for shape, dtype in outs),
        in_specs=specs + [VMEM] * (len(operands) - len(specs)),
        out_specs=(VMEM,) * len(outs),
        scratch_shapes=scratch,
        compiler_params=pltpu.CompilerParams(vmem_limit_bytes=16 << 20),
        cost_estimate=pl.CostEstimate(flops=1 << 20, bytes_accessed=cost, transcendentals=0),
        name=name,
    )(
        *(
            pltpu.with_memory_space_constraint(operand, pltpu.HBM) if spec is HBM else operand
            for spec, operand in zip(specs + [VMEM] * len(operands), operands)
        )
    )


def four_cols(
    pair, out_grad, pair_bias, w_query, w_key, w_value, w_gate, w_out, tile_mask, chain_ids
):
    col_index = lax.axis_index("col")
    head_index = lax.axis_index("head")
    col = col_index.reshape(1)
    width, keys, wide = 2 * HD, 4 * TILE, 2 * TILE
    x = pair.reshape(TILE, C)
    head = head_index.reshape(1)
    x_direct = exchange(x, staggered(far_col, end_col))
    x_next = exchange(x, next_col)
    x, grad, w_qg, w_kv, bias, left, right, gate_t, gated_grad_t = on_core(
        local_kernel, "local", [SMEM] + [HBM] * 10,
        (
            col, tile_mask, x, out_grad.reshape(TILE, C), pair_bias, chain_ids.reshape(4, TILE),
            w_query.T, w_key.T, w_value.T, w_gate.T, w_out,
        ),
        (
            ((TILE, C), BF16), ((TILE, C), BF16), ((2 * width, C), BF16), ((2 * width, C), BF16),
            ((keys, wide), F32), ((C, 2 * wide), BF16), ((2 * wide, C), BF16),
            ((width, TILE), F32), ((width, TILE), F32),
        ),
        [
            pltpu.SMEM((4, 4), jnp.int32), pltpu.VMEM((4, TILE), jnp.int32),
            pltpu.VMEM((width, C), BF16), pltpu.VMEM((TILE, 2, keys), BF16),
            pltpu.SemaphoreType.DMA((10,)),
        ],
    )
    x_direct, w_kv = lax.optimization_barrier((x_direct, w_kv))
    x_crossed = exchange(x_direct, other_head)
    raw, local, key_value_grad = on_core(
        attention_kernel, "attention", [SMEM, SMEM],
        (col, head, x, x_next, x_direct, x_crossed, grad, bias, left, right, gate_t, gated_grad_t, w_kv),
        (((5 * width, C), BF16), ((TILE, C), BF16), ((keys, C), BF16)),
        [
            pltpu.VMEM((keys, C), BF16), pltpu.VMEM((keys, 2 * wide), F32),
            pltpu.VMEM((keys, wide), BF16), pltpu.VMEM((keys, 2 * wide), BF16),
        ],
    )

    def summed(one, two):
        return (one.astype(F32) + two.astype(F32)).astype(BF16)

    keep, send = on_core(
        parts_kernel, "parts", [SMEM, SMEM], (col, head, key_value_grad, local, w_qg, w_kv),
        (((wide, C), F32), ((wide, C), BF16)), [pltpu.VMEM((keys, C), F32)],
    )
    half = TILE // 2
    raw = summed(raw, exchange(raw, staggered(next_col, far_col)))
    given = exchange(send, other_head)
    keep, send = on_core(
        fold_kernel, "fold_heads", [], (keep, given), (((TILE, C), F32), ((TILE, C), BF16)),
    )
    raw, keep = lax.optimization_barrier((raw, keep))
    given = exchange(send, next_col)
    send = (keep[half:] + given[half:].astype(F32)).astype(BF16)
    keep, early = keep[:half], given[:half]
    raw = summed(raw, exchange(raw, staggered(far_col, other_row)))
    raw, keep = lax.optimization_barrier((raw, keep))
    given = exchange(send, far_col)
    keep = keep + early.astype(F32)
    last = exchange(raw, staggered(other_row, next_col))
    total, squares = on_core(
        squares_kernel, "squares", [], (raw, last), (((5 * width, C), F32), ((8, C), F32)),
    )
    grads = on_core(
        clip_kernel, "clip", [], (total, squares, exchange(squares, other_head), keep, given),
        (((width, C), F32),) * 5 + (((half, C), BF16),),
    )
    query_grad, gate_grad, key_grad, value_grad, out_weight_grad, pair_grad = grads
    return (
        pair_grad.reshape(1, half, C),
        query_grad.T,
        key_grad.T,
        value_grad.T,
        gate_grad.T,
        out_weight_grad,
    )


def per_device(pair, out_grad, pair_bias, *rest):
    small = lax.axis_size("col") == 4 and lax.axis_size("row") == 2 and lax.axis_size("head") == 2
    if small and pair.shape == (1, TILE, C) and pair_bias.shape == (TILE, 2, 4 * TILE):
        return four_cols(pair, out_grad, pair_bias, *rest)
    return any_cols(pair, out_grad, pair_bias, *rest)


def solution(mesh):
    return jax.shard_map(
        per_device,
        mesh=mesh,
        in_specs=(
            P(("groups", "row"), "col", None),
            P(("groups", "row"), "col", None),
            P(("groups", "col"), "head", None),
            P(None, "head"),
            P(None, "head"),
            P(None, "head"),
            P(None, "head"),
            P("head", None),
            P("groups", None),
            P("groups"),
        ),
        out_specs=(
            P(("groups", "row"), ("col", "head"), None),
            P("groups", "head"),
            P("groups", "head"),
            P("groups", "head"),
            P("groups", "head"),
            P(("groups", "head"), None),
        ),
        check_vma=False,
    )
```

```python
import math

import jax
import jax.numpy as jnp
from jax import lax
from jax.experimental import pallas as pl
from jax.experimental.pallas import tpu as pltpu
from jax.sharding import PartitionSpec as P

C = 128
H = 4
HD = 32
TILE = 128


NEG_FILL = -1e30
F32 = jnp.float32
BF16 = jnp.bfloat16
CLIP_NORM = 0.5 * math.sqrt(5.0 * C * H * HD)


def shifted(value, axis, steps):
    count = lax.axis_size(axis)
    pairs = [(source, (source + steps) % count) for source in range(count)]
    return lax.ppermute(value, axis, pairs)


def allowed_between(tile_mask, chain_ids, query_start, query_count, key_start, key_count):
    tile_ids = jnp.arange(tile_mask.shape[0], dtype=jnp.int32)
    query_pos = query_start + jnp.arange(query_count, dtype=jnp.int32)
    key_pos = key_start + jnp.arange(key_count, dtype=jnp.int32)
    query_tiles = (query_pos[:, None] // TILE == tile_ids[None, :]).astype(jnp.float32)
    key_tiles = (key_pos[:, None] // TILE == tile_ids[None, :]).astype(jnp.float32)
    marks = jnp.dot(jnp.dot(query_tiles, tile_mask.astype(jnp.float32)), key_tiles.T)
    query_chain = lax.dynamic_slice_in_dim(chain_ids, query_start, query_count)
    key_chain = lax.dynamic_slice_in_dim(chain_ids, key_start, key_count)
    return (marks > 0.5) | (query_chain[:, None] == key_chain[None, :])


def score_block(query_four, key_four, bias_block, allowed):
    scores = jnp.einsum("rjhd,rkhd->rjhk", query_four, key_four, preferred_element_type=jnp.float32)
    scores = scores + bias_block[None].astype(jnp.float32)
    return jnp.where(allowed[None, :, None, :], scores, NEG_FILL)


def prob_and_grad(
    query_four, grad_four, log_total, delta_sum, key_four, value_four, bias_block, allowed
):
    scores = score_block(query_four, key_four, bias_block, allowed)
    prob = jnp.where(allowed[None, :, None, :], jnp.exp(scores - log_total[..., None]), 0.0)
    grad_prob = jnp.einsum(
        "rjhd,rkhd->rjhk", grad_four, value_four, preferred_element_type=jnp.float32
    )
    grad_score = (prob * (grad_prob - delta_sum[..., None])).astype(jnp.bfloat16)
    return (prob.astype(jnp.bfloat16), grad_score)


def any_cols(
    pair, out_grad, pair_bias, w_query, w_key, w_value, w_gate, w_out, tile_mask, chain_ids
):
    rows_dev, cols_dev, channels = pair.shape
    heads_dev = pair_bias.shape[1]
    head_width = w_query.shape[1]
    head_size = head_width // heads_dev
    hd_scale = head_size ** (-0.5)
    col_count = lax.axis_size("col")
    col_index = lax.axis_index("col")
    col_start = col_index * cols_dev
    shape_four = (rows_dev, cols_dev, heads_dev, head_size)
    stat_shape = (rows_dev, cols_dev, heads_dev)
    flat_pair = pair.reshape(rows_dev * cols_dev, channels)
    flat_grad = out_grad.reshape(rows_dev * cols_dev, channels)
    w_joined = jnp.concatenate([w_query, w_key, w_value, w_gate], axis=1)
    projected = jnp.dot(flat_pair, w_joined, preferred_element_type=jnp.float32)
    query_flat = (projected[:, :head_width] * hd_scale).astype(jnp.bfloat16)
    key_grid = (
        projected[:, head_width : 2 * head_width]
        .astype(jnp.bfloat16)
        .reshape(rows_dev, cols_dev, head_width)
    )
    value_grid = (
        projected[:, 2 * head_width : 3 * head_width]
        .astype(jnp.bfloat16)
        .reshape(rows_dev, cols_dev, head_width)
    )
    gate_value = jax.nn.sigmoid(projected[:, 3 * head_width :])
    query_four = query_flat.reshape(shape_four)
    key_piece = lax.all_gather(key_grid, "col", axis=1, tiled=True)
    value_piece = lax.all_gather(value_grid, "col", axis=1, tiled=True)
    key_count = key_piece.shape[1]
    allowed = allowed_between(tile_mask, chain_ids, col_start, cols_dev, jnp.int32(0), key_count)
    bias_block = pair_bias
    run_max = jnp.full(stat_shape, NEG_FILL, jnp.float32)
    key_four = key_piece.reshape(rows_dev, key_count, heads_dev, head_size)
    value_four = value_piece.reshape(rows_dev, key_count, heads_dev, head_size)
    scores = score_block(query_four, key_four, bias_block, allowed)
    new_max = jnp.maximum(run_max, jnp.max(scores, axis=3))
    weights = jnp.where(allowed[None, :, None, :], jnp.exp(scores - new_max[..., None]), 0.0)
    new_sum = jnp.sum(weights, axis=3)
    added = jnp.einsum(
        "rjhk,rkhd->rjhd",
        weights.astype(jnp.bfloat16),
        value_four,
        preferred_element_type=jnp.float32,
    )
    attended = (added / new_sum[..., None]).reshape(rows_dev * cols_dev, head_width)
    log_total = new_max + jnp.log(new_sum)
    gated = (gate_value * attended).astype(jnp.bfloat16)
    grad_gated = jnp.dot(flat_grad, w_out.T, preferred_element_type=jnp.float32)
    grad_att = (grad_gated * gate_value).astype(jnp.bfloat16)
    grad_gate_logit = (grad_gated * attended * gate_value * (1.0 - gate_value)).astype(jnp.bfloat16)
    delta_sum = jnp.sum((grad_att.astype(jnp.float32) * attended).reshape(shape_four), axis=3)
    grad_four = grad_att.reshape(shape_four)

    def back_turn(turn_index, loop_state):
        travel_keys, travel_grads, query_acc = loop_state
        owner_col = jnp.mod(col_index - turn_index, col_count)
        key_start = owner_col * cols_dev
        allowed = allowed_between(tile_mask, chain_ids, col_start, cols_dev, key_start, cols_dev)
        bias_block = lax.dynamic_slice_in_dim(pair_bias, key_start, cols_dev, 2)
        grads_in = travel_grads
        query_in = query_acc
        key_four = travel_keys[0].reshape(shape_four)
        value_four = travel_keys[1].reshape(shape_four)
        prob_bf, grad_score = prob_and_grad(
            query_four, grad_four, log_total, delta_sum, key_four, value_four, bias_block, allowed
        )
        query_more = jnp.einsum(
            "rjhk,rkhd->rjhd", grad_score, key_four, preferred_element_type=jnp.float32
        )
        key_more = jnp.einsum(
            "rjhk,rjhd->rkhd", grad_score, query_four, preferred_element_type=jnp.float32
        )
        value_more = jnp.einsum(
            "rjhk,rjhd->rkhd", prob_bf, grad_four, preferred_element_type=jnp.float32
        )
        travel_grads = grads_in + jnp.stack([key_more, value_more]).reshape(grads_in.shape)
        query_acc = query_in + query_more
        travel_keys = shifted(travel_keys, "col", 1)
        travel_grads = shifted(travel_grads.astype(jnp.bfloat16), "col", 1).astype(
            travel_grads.dtype
        )
        return (travel_keys, travel_grads, query_acc)

    def back_pair(pair_index, loop_state):
        for half_turn in range(2):
            loop_state = back_turn(2 * pair_index + half_turn, loop_state)
        return loop_state

    loop_start = (
        jnp.stack([key_grid, value_grid]),
        jnp.zeros((2, rows_dev, cols_dev, head_width), jnp.float32),
        jnp.zeros(shape_four, jnp.float32),
    )
    travel_keys, key_value_acc, query_acc = lax.fori_loop(0, col_count // 2, back_pair, loop_start)
    query_grad = (
        (query_acc * hd_scale).astype(jnp.bfloat16).reshape(rows_dev * cols_dev, head_width)
    )
    key_grad = key_value_acc[0].astype(jnp.bfloat16).reshape(rows_dev * cols_dev, head_width)
    value_grad = key_value_acc[1].astype(jnp.bfloat16).reshape(rows_dev * cols_dev, head_width)
    grad_joined = jnp.concatenate([query_grad, key_grad, value_grad, grad_gate_logit], axis=1)
    partial_pair = jnp.dot(grad_joined, w_joined.T, preferred_element_type=jnp.float32).reshape(
        rows_dev, cols_dev, channels
    )
    pair_grad = lax.psum_scatter(
        partial_pair.astype(jnp.bfloat16), "head", scatter_dimension=1, tiled=True
    )
    raw_four = jnp.dot(flat_pair.T, grad_joined, preferred_element_type=jnp.float32)
    raw_out = jnp.dot(gated.T, flat_grad, preferred_element_type=jnp.float32)
    summed_four, summed_out = lax.psum((raw_four, raw_out), ("col", "row"))
    local_squares = jnp.sum(summed_four * summed_four) + jnp.sum(summed_out * summed_out)
    squares = lax.psum(local_squares, "head")
    clip = jnp.minimum(1.0, 0.5 * math.sqrt(5.0 * C * H * HD) / jnp.sqrt(squares + 1e-06))
    return (
        pair_grad,
        summed_four[:, :head_width] * clip,
        summed_four[:, head_width : 2 * head_width] * clip,
        summed_four[:, 2 * head_width : 3 * head_width] * clip,
        summed_four[:, 3 * head_width :] * clip,
        summed_out * clip,
    )


def exchange(value, partner):
    cols, rows, heads = lax.axis_size("col"), lax.axis_size("row"), lax.axis_size("head")
    pairs = []
    for col in range(cols):
        for row in range(rows):
            for head in range(heads):
                to_col, to_row, to_head = partner(col, row, head)
                source = (col * rows + row) * heads + head
                pairs.append((source, (to_col * rows + to_row) * heads + to_head))
    return lax.ppermute(value, ("col", "row", "head"), pairs)


def next_col(col, row, head):
    return col ^ 1, row, head


def far_col(col, row, head):
    return col ^ 2, row, head


def end_col(col, row, head):
    return col ^ 3, row, head


def other_row(col, row, head):
    return col, row ^ 1, head


def other_head(col, row, head):
    return col, row, head ^ 1


def staggered(first, second):
    return lambda col, row, head: (first, second)[head](col, row, head)


def dot_nn(left, right):
    return jnp.dot(left, right, preferred_element_type=F32)


def dot_nt(left, right):
    return lax.dot_general(left, right, (((1,), (1,)), ((), ())), preferred_element_type=F32)


def split_rows(flat):
    first = lax.broadcasted_iota(jnp.int32, flat.shape, 0) < HD
    zero = jnp.zeros_like(flat)
    return jnp.concatenate([jnp.where(first, flat, zero), jnp.where(first, zero, flat)], axis=1)


def join_rows(wide):
    count = wide.shape[1] // 2
    first = lax.broadcasted_iota(jnp.int32, (wide.shape[0], count), 0) < HD
    return jnp.where(first, wide[:, :count], wide[:, count:])


def split_cols(flat):
    first = lax.broadcasted_iota(jnp.int32, flat.shape, 1) < HD
    zero = jnp.zeros_like(flat)
    return jnp.concatenate([jnp.where(first, flat, zero), jnp.where(first, zero, flat)], axis=0)


def local_kernel(
    col_ref, tile_hbm, x_hbm, grad_hbm, bias_hbm, chain_hbm, wq_hbm, wk_hbm, wv_hbm, wg_hbm, wo_hbm,
    x_ref, grad_ref, w_qg_ref, w_kv_ref, bias_out, left_out, right_out, gate_out, gated_grad_out,
    tile_ref, chain_ref, wo_ref, bias_ref, sems,
):
    scale = HD ** (-0.5)
    width = 2 * TILE
    me = col_ref[0]
    moves = [
        (x_hbm, x_ref),
        (wq_hbm, w_qg_ref.at[: 2 * HD]),
        (wg_hbm, w_qg_ref.at[2 * HD :]),
        (grad_hbm, grad_ref),
        (wo_hbm, wo_ref),
        (chain_hbm, chain_ref),
        (tile_hbm, tile_ref),
        (bias_hbm, bias_ref),
        (wk_hbm, w_kv_ref.at[: 2 * HD]),
        (wv_hbm, w_kv_ref.at[2 * HD :]),
    ]
    copies = [
        pltpu.make_async_copy(source, target, sems.at[place])
        for place, (source, target) in enumerate(moves)
    ]
    for copy in copies:
        copy.start()
    for copy in copies[:5]:
        copy.wait()
    x = x_ref[...]
    query_gate = dot_nt(w_qg_ref[...], x)
    gated_grad_t = dot_nt(wo_ref[...], grad_ref[...])
    query = (dot_nt(x, w_qg_ref[: 2 * HD, :]) * scale).astype(BF16)
    query_t = (query_gate[: 2 * HD] * scale).astype(BF16)
    gate_t = jax.nn.sigmoid(query_gate[2 * HD :])
    att_grad_t = (gated_grad_t * gate_t).astype(BF16)
    att_grad_f = att_grad_t.astype(F32)
    att_grad = jnp.transpose(att_grad_f).astype(BF16)
    zero_wide = jnp.zeros((2 * HD, width), BF16)
    zero_tall = jnp.zeros((width, 2 * HD), BF16)
    left_out[: 2 * HD, :] = jnp.concatenate([split_rows(query_t), zero_wide], axis=1)
    left_out[2 * HD :, :] = jnp.concatenate([zero_wide, split_rows(att_grad_t)], axis=1)
    right_out[:width, :] = jnp.concatenate([split_cols(query), zero_tall], axis=1)
    right_out[width:, :] = jnp.concatenate([zero_tall, split_cols(att_grad)], axis=1)
    gate_out[...] = gate_t
    gated_grad_out[...] = gated_grad_t
    for copy in copies[5:]:
        copy.wait()
    chains = chain_ref[...].astype(F32)
    own_chain = chain_ref[pl.ds(me, 1), :].astype(F32)
    for block in range(4):
        rows = slice(block * TILE, (block + 1) * TILE)
        key_chain = jnp.transpose(jnp.broadcast_to(chains[block : block + 1, :], (TILE, TILE)))
        apart = jnp.where(tile_ref[me, block] == 1, 0.0, 1.0)
        banned = jnp.where(key_chain == own_chain, 0.0, apart) > 0.5
        for head in range(2):
            bias = bias_ref[:, head, rows].astype(F32)
            bias_out[rows, head * TILE : (head + 1) * TILE] = jnp.where(
                banned, NEG_FILL, jnp.transpose(bias)
            )


def attention_kernel(
    col_ref, head_ref, x_ref, next_ref, direct_ref, crossed_ref, grad_ref, bias_ref, left_ref, right_ref,
    gate_ref, gated_grad_ref, w_kv_ref,
    raw_ref, local_ref, key_value_grad_ref,
    pairs_ref, scores_ref, expo_ref, both_ref,
):
    scale = HD ** (-0.5)
    width = 2 * TILE
    me, head = col_ref[0], head_ref[0]
    for bits, ref in ((0, x_ref), (1, next_ref), (2 + head, direct_ref), (3 - head, crossed_ref)):
        place = pl.multiple_of(lax.bitwise_xor(me, bits) * TILE, TILE)
        pairs_ref[pl.ds(place, TILE), :] = ref[...]
    w_kv = w_kv_ref[...]
    pairs = pairs_ref[...]
    key_value = dot_nt(pairs, w_kv).astype(BF16)
    key_value_t = dot_nt(w_kv, pairs).astype(BF16)
    left = left_ref[...]
    top = None
    for block in range(4):
        rows = slice(block * TILE, (block + 1) * TILE)
        product = dot_nn(key_value[rows], left)
        scores = product[:, :width] + bias_ref[rows, :]
        scores_ref[rows, :width] = scores
        scores_ref[rows, width:] = product[:, width:]
        part = jnp.max(scores.reshape(TILE // 8, 8, width), axis=0)
        top = part if top is None else jnp.maximum(top, part)
    top = jnp.max(top, axis=0, keepdims=True)
    total = jnp.zeros((8, width), F32)
    weighted = jnp.zeros((8, width), F32)
    for block in range(4):
        rows = slice(block * TILE, (block + 1) * TILE)
        expo = jnp.exp(scores_ref[rows, :width] - top)
        scores_ref[rows, :width] = expo
        expo_ref[rows, :] = expo.astype(BF16)
        total = total + jnp.sum(expo.reshape(TILE // 8, 8, width), axis=0)
        products = expo * scores_ref[rows, width:]
        weighted = weighted + jnp.sum(products.reshape(TILE // 8, 8, width), axis=0)
    inverse = 1.0 / jnp.sum(total, axis=0, keepdims=True)
    delta = jnp.sum(weighted, axis=0, keepdims=True) * inverse
    attended_t = join_rows(dot_nn(key_value_t[2 * HD :], expo_ref[...]) * inverse)
    gate_t, gated_grad_t = gate_ref[...], gated_grad_ref[...]
    gated_t = (gate_t * attended_t).astype(BF16)
    gate_logit_t = gated_grad_t * attended_t * gate_t * (1.0 - gate_t)
    for block in range(4):
        rows = slice(block * TILE, (block + 1) * TILE)
        prob = scores_ref[rows, :width] * inverse
        both_ref[rows, :width] = (prob * (scores_ref[rows, width:] - delta)).astype(BF16)
        both_ref[rows, width:] = prob.astype(BF16)
    query_grad_t = join_rows(dot_nn(key_value_t[: 2 * HD], both_ref[:, :width])) * scale
    key_value_grad = dot_nn(both_ref[...], right_ref[...])
    local_t = jnp.concatenate([query_grad_t, gate_logit_t], axis=0)
    local_ref[...] = jnp.transpose(local_t).astype(BF16)
    key_value_grad_ref[...] = key_value_grad.astype(BF16)
    raw_ref[: 4 * HD, :] = dot_nn(local_t.astype(BF16), x_ref[...]).astype(BF16)
    raw_ref[4 * HD : 8 * HD, :] = dot_nn(jnp.transpose(key_value_grad).astype(BF16), pairs).astype(BF16)
    raw_ref[8 * HD :, :] = dot_nn(gated_t, grad_ref[...]).astype(BF16)


def parts_kernel(
    col_ref, head_ref, key_value_grad_ref, local_ref, w_qg_ref, w_kv_ref, keep_ref, send_ref, parts_ref
):
    me, head = col_ref[0], head_ref[0]
    half = TILE // 2
    parts_ref[...] = dot_nn(key_value_grad_ref[...], w_kv_ref[...])
    own = pl.ds(pl.multiple_of(me * TILE, TILE), TILE)
    parts_ref[own, :] = parts_ref[own, :] + dot_nn(local_ref[...], w_qg_ref[...])
    for place, bits in enumerate((0, 2, 1, 3)):
        start = lax.bitwise_xor(me, bits) * TILE
        mine = pl.multiple_of(start + head * half, half)
        other = pl.multiple_of(start + (1 - head) * half, half)
        rows = slice(place * half, (place + 1) * half)
        keep_ref[rows, :] = parts_ref[pl.ds(mine, half), :]
        send_ref[rows, :] = parts_ref[pl.ds(other, half), :].astype(BF16)


def fold_kernel(own_ref, other_ref, keep_ref, send_ref):
    half = keep_ref.shape[0]
    keep_ref[...] = own_ref[:half, :] + other_ref[:half, :].astype(F32)
    send_ref[...] = (own_ref[half:, :] + other_ref[half:, :].astype(F32)).astype(BF16)


def squares_kernel(own_ref, other_ref, total_ref, squares_ref):
    total = own_ref[...].astype(F32) + other_ref[...].astype(F32)
    total_ref[...] = total
    squares_ref[...] = jnp.sum((total * total).reshape(total.shape[0] // 8, 8, C), axis=0)


def clip_kernel(
    total_ref, own_ref, other_ref, pair_own_ref, pair_other_ref,
    query_ref, gate_ref, key_ref, value_ref, out_ref, pair_ref,
):
    squares = own_ref[...] + other_ref[...]
    squares = jnp.sum(jnp.sum(squares, axis=0, keepdims=True), axis=1, keepdims=True)
    clip = jnp.minimum(1.0, CLIP_NORM / jnp.sqrt(squares + 1e-06))
    for part, ref in enumerate((query_ref, gate_ref, key_ref, value_ref, out_ref)):
        ref[...] = total_ref[part * 2 * HD : (part + 1) * 2 * HD, :] * clip
    pair_ref[...] = (pair_own_ref[...] + pair_other_ref[...].astype(F32)).astype(BF16)


VMEM = pl.BlockSpec(memory_space=pltpu.VMEM)
SMEM = pl.BlockSpec(memory_space=pltpu.SMEM)
HBM = pl.BlockSpec(memory_space=pltpu.HBM)


def on_core(kernel, name, specs, operands, outs, scratch=(), cost=1 << 18):
    return pl.pallas_call(
        kernel,
        out_shape=tuple(jax.ShapeDtypeStruct(shape, dtype) for shape, dtype in outs),
        in_specs=specs + [VMEM] * (len(operands) - len(specs)),
        out_specs=(VMEM,) * len(outs),
        scratch_shapes=scratch,
        compiler_params=pltpu.CompilerParams(vmem_limit_bytes=16 << 20),
        cost_estimate=pl.CostEstimate(flops=1 << 20, bytes_accessed=cost, transcendentals=0),
        name=name,
    )(
        *(
            pltpu.with_memory_space_constraint(operand, pltpu.HBM) if spec is HBM else operand
            for spec, operand in zip(specs + [VMEM] * len(operands), operands)
        )
    )


def four_cols(
    pair, out_grad, pair_bias, w_query, w_key, w_value, w_gate, w_out, tile_mask, chain_ids
):
    col_index = lax.axis_index("col")
    head_index = lax.axis_index("head")
    col = col_index.reshape(1)
    width, keys, wide = 2 * HD, 4 * TILE, 2 * TILE
    x = pair.reshape(TILE, C)
    head = head_index.reshape(1)
    x_direct = exchange(x, staggered(far_col, end_col))
    x_next = exchange(x, next_col)
    x, grad, w_qg, w_kv, bias, left, right, gate_t, gated_grad_t = on_core(
        local_kernel, "local", [SMEM] + [HBM] * 10,
        (
            col, tile_mask, x, out_grad.reshape(TILE, C), pair_bias, chain_ids.reshape(4, TILE),
            w_query.T, w_key.T, w_value.T, w_gate.T, w_out,
        ),
        (
            ((TILE, C), BF16), ((TILE, C), BF16), ((2 * width, C), BF16), ((2 * width, C), BF16),
            ((keys, wide), F32), ((C, 2 * wide), BF16), ((2 * wide, C), BF16),
            ((width, TILE), F32), ((width, TILE), F32),
        ),
        [
            pltpu.SMEM((4, 4), jnp.int32), pltpu.VMEM((4, TILE), jnp.int32),
            pltpu.VMEM((width, C), BF16), pltpu.VMEM((TILE, 2, keys), BF16),
            pltpu.SemaphoreType.DMA((10,)),
        ],
    )
    x_direct, w_kv = lax.optimization_barrier((x_direct, w_kv))
    x_crossed = exchange(x_direct, other_head)
    raw, local, key_value_grad = on_core(
        attention_kernel, "attention", [SMEM, SMEM],
        (col, head, x, x_next, x_direct, x_crossed, grad, bias, left, right, gate_t, gated_grad_t, w_kv),
        (((5 * width, C), BF16), ((TILE, C), BF16), ((keys, C), BF16)),
        [
            pltpu.VMEM((keys, C), BF16), pltpu.VMEM((keys, 2 * wide), F32),
            pltpu.VMEM((keys, wide), BF16), pltpu.VMEM((keys, 2 * wide), BF16),
        ],
    )

    def summed(one, two):
        return (one.astype(F32) + two.astype(F32)).astype(BF16)

    keep, send = on_core(
        parts_kernel, "parts", [SMEM, SMEM], (col, head, key_value_grad, local, w_qg, w_kv),
        (((wide, C), F32), ((wide, C), BF16)), [pltpu.VMEM((keys, C), F32)],
    )
    half = TILE // 2
    raw = summed(raw, exchange(raw, staggered(other_row, next_col)))
    given = exchange(send, other_head)
    keep, send = on_core(
        fold_kernel, "fold_heads", [], (keep, given), (((TILE, C), F32), ((TILE, C), BF16)),
    )
    raw, keep = lax.optimization_barrier((raw, keep))
    given = exchange(send, next_col)
    send = (keep[half:] + given[half:].astype(F32)).astype(BF16)
    keep, early = keep[:half], given[:half]
    raw = summed(raw, exchange(raw, staggered(far_col, other_row)))
    raw, keep = lax.optimization_barrier((raw, keep))
    given = exchange(send, far_col)
    keep = keep + early.astype(F32)
    last = exchange(raw, staggered(next_col, far_col))
    total, squares = on_core(
        squares_kernel, "squares", [], (raw, last), (((5 * width, C), F32), ((8, C), F32)),
    )
    grads = on_core(
        clip_kernel, "clip", [], (total, squares, exchange(squares, other_head), keep, given),
        (((width, C), F32),) * 5 + (((half, C), BF16),),
    )
    query_grad, gate_grad, key_grad, value_grad, out_weight_grad, pair_grad = grads
    return (
        pair_grad.reshape(1, half, C),
        query_grad.T,
        key_grad.T,
        value_grad.T,
        gate_grad.T,
        out_weight_grad,
    )


def per_device(pair, out_grad, pair_bias, *rest):
    small = lax.axis_size("col") == 4 and lax.axis_size("row") == 2 and lax.axis_size("head") == 2
    if small and pair.shape == (1, TILE, C) and pair_bias.shape == (TILE, 2, 4 * TILE):
        return four_cols(pair, out_grad, pair_bias, *rest)
    return any_cols(pair, out_grad, pair_bias, *rest)


def solution(mesh):
    return jax.shard_map(
        per_device,
        mesh=mesh,
        in_specs=(
            P(("groups", "row"), "col", None),
            P(("groups", "row"), "col", None),
            P(("groups", "col"), "head", None),
            P(None, "head"),
            P(None, "head"),
            P(None, "head"),
            P(None, "head"),
            P("head", None),
            P("groups", None),
            P("groups"),
        ),
        out_specs=(
            P(("groups", "row"), ("col", "head"), None),
            P("groups", "head"),
            P("groups", "head"),
            P("groups", "head"),
            P("groups", "head"),
            P(("groups", "head"), None),
        ),
        check_vma=False,
    )
```
